256 devices in a mesh: slab: 32 (over x, z), col: 8 (over y, core).
Axes of the slice: x: 4, y: 4, z: 8, core: 2. Of those that a mesh axis runs over, the one named last changes fastest.
Arguments:
- order_params: float32 [16, 256, 64, 256], P(None, 'slab', 'col'), may hold values from 0 to 0.5
- layer_mask: int32 [256, 64, 256], P('slab', 'col'), may hold values 0 or 1
- coarse_temp: float32 [192, 32, 128], P('slab', 'col'), may hold values from 0.5 to 1.5, as said below
- coarse_rows: int32 [32], replicated, may hold values from 2 to 6, as said below
- grain_ids: int32 [32, 8, 16], replicated, may hold values from 0 to 2207, as said below
- energy: float32 [2208], replicated, may hold values from 0.5 to 6
Outputs:
- evolved: float32 [16, 256, 64, 256], P(None, 'slab', 'col')
The draws below stay inside these ranges and needn't reach their ends.
Inputs may be any that keep to these rules, and one draw needn't show every extreme that they name: coarse_rows sums to 128; the s-th block of coarse planes begins within 1 planes of s * 4; some entry equals 6. `coarse_temp`: rows of one index of slab past its entry of coarse_rows are not part of the field. `grain_ids`: the 16 ids of a block are distinct; a block shares exactly 4 ids with each block beside it along slab and along col and none with any other block.
All inputs are finite; a program needn't handle non-finite values. No bound on the sum of `layer_mask` on one device may be relied on, other than what follows from the above.
Results may differ from the reference program's by a relative error of at most 0.0001.
Values sent between devices are 32-bit elements; how exact they have to be, the bound alone decides.
A program may use at most 64 MiB of HBM per device.

```python
import math
import jax
import jax.numpy as jnp
from jax import lax

Q = 16
SHARE = 4
JITTER = 1
STEPS = 4
CX = 8
CY = 8
CAPX = 6
FINE_CELLS_TRACK = 256
FINE_CELLS_ACROSS = 64
FINE_CELLS_HEIGHT = 256
NXC = 128
NYC = 32
NZC = 128
GRAINS = 2208
N_SLAB = 32
N_COL = 8


def draw_coarse_temp(key, part):
    row_total = N_SLAB * CAPX
    owner = (jnp.arange(row_total) // CAPX).astype(jnp.float32)
    trend = 0.7 + 0.6 * owner / (N_SLAB - 1)
    first_key = jax.random.fold_in(key, 0)
    noise = jax.random.uniform(first_key, (row_total, NYC, NZC), jnp.float32, -0.2, 0.2)
    return (trend[:, None, None] + noise).astype(jnp.float32)


def draw_coarse_rows(key, part):
    first_key, second_key = jax.random.split(key)
    offsets = jax.random.randint(first_key, (N_SLAB + 1,), -JITTER, JITTER + 1)
    chosen = jax.random.randint(second_key, (), 1, N_SLAB - 1)
    offsets = offsets.at[chosen].set(-JITTER).at[chosen + 1].set(JITTER)
    offsets = offsets.at[0].set(0).at[N_SLAB].set(0)
    return (CX // 2 + offsets[1:] - offsets[:-1]).astype(jnp.int32)


def draw_grain_ids(key, part):
    first_key, second_key = jax.random.split(key)
    slab_index = jnp.arange(N_SLAB)[:, None, None]
    col_index = jnp.arange(N_COL)[None, :, None]
    rank_index = jnp.arange(SHARE)[None, None, :]
    across_count = (N_SLAB + 1) * N_COL * SHARE
    low_x = (slab_index * N_COL + col_index) * SHARE + rank_index
    high_x = ((slab_index + 1) * N_COL + col_index) * SHARE + rank_index
    low_y = across_count + (slab_index * (N_COL + 1) + col_index) * SHARE + rank_index
    high_y = across_count + (slab_index * (N_COL + 1) + col_index + 1) * SHARE + rank_index
    full_shape = (N_SLAB, N_COL, SHARE)
    grain_table = jnp.concatenate([jnp.broadcast_to(low_x, full_shape), jnp.broadcast_to(high_x, full_shape), jnp.broadcast_to(low_y, full_shape), jnp.broadcast_to(high_y, full_shape)], axis=-1)
    relabel = jax.random.permutation(first_key, GRAINS)
    grain_table = relabel[grain_table]
    scores = jax.random.randint(second_key, (N_SLAB, N_COL, Q), 0, 1 << 20) * Q + jnp.arange(Q)[None, None, :]
    slot_order = jnp.argsort(scores, axis=-1)
    return jnp.take_along_axis(grain_table, slot_order, axis=-1).astype(jnp.int32)


def plant(result, rng, low, largest):
    longest = result.shape.index(max(result.shape))
    spots = []
    for shift in (0, 1):
        where = [jax.random.randint(jax.random.fold_in(rng, axis), (), 0, length) for axis, length in enumerate(result.shape)]
        where[longest] = (where[longest] + shift) % result.shape[longest]
        spots.append(tuple(where))
    return result.at[spots[0]].set(low).at[spots[1]].set(largest)


def levels(rng, shape, pieces, low, high):
    loudness, own = 1.0, jax.random.fold_in(rng, 6)
    for position, blocks in pieces:
        draws = jnp.exp(jax.random.uniform(jax.random.fold_in(own, position), (blocks,), jnp.float32, low / len(pieces), high / len(pieces)))
        loudness = loudness * jnp.repeat(draws, shape[position] // blocks).reshape([-1 if axis == position else 1 for axis in range(len(shape))])
    return loudness


def setup_inputs(seed: int = 0) -> dict:
    splits = jax.random.split(jax.random.key(seed), 7)
    order_params = jnp.clip(0.5 * jax.random.uniform(splits[0], (Q, FINE_CELLS_TRACK, FINE_CELLS_ACROSS, FINE_CELLS_HEIGHT), jnp.float32) ** levels(splits[0], (Q, FINE_CELLS_TRACK, FINE_CELLS_ACROSS, FINE_CELLS_HEIGHT), ((1, 32), (2, 8)), -0.2, 0.2), 0.0, 0.5)
    layer_mask = plant((jax.random.randint(splits[1], (FINE_CELLS_TRACK, FINE_CELLS_ACROSS, FINE_CELLS_HEIGHT), 0, 4) < 3).astype(jnp.int32), jax.random.fold_in(splits[1], 1), 0, 1)
    coarse_temp = draw_coarse_temp(jax.random.fold_in(splits[6], 71), 0)
    coarse_rows = draw_coarse_rows(jax.random.fold_in(splits[6], 71), 0)
    grain_ids = draw_grain_ids(jax.random.fold_in(splits[6], 71), 0)
    energy = jnp.clip(jnp.exp(jax.random.uniform(splits[5], (GRAINS,), jnp.float32, math.log(0.5), math.log(6.0))), 0.5, 6.0)
    return {"order_params": order_params, "layer_mask": layer_mask, "coarse_temp": coarse_temp, "coarse_rows": coarse_rows, "grain_ids": grain_ids, "energy": energy}


FULL_ACCURACY = lax.Precision.HIGHEST
TIME_STEP = 0.05
COUPLING = 1.5


def linear_resample_axis(values, axis, fine_count):
    coarse_count = values.shape[axis]
    fine_index = jnp.arange(fine_count, dtype=jnp.int32)
    lower_index = (2 * fine_index - 1) // 4
    weight = ((2 * fine_index - 1) - 4 * lower_index).astype(jnp.float32) / 4.0
    lower_node = jnp.clip(lower_index, 0, coarse_count - 1).astype(jnp.int32)
    upper_node = jnp.clip(lower_index + 1, 0, coarse_count - 1).astype(jnp.int32)
    lower_values = jnp.take(values, lower_node, axis=axis)
    upper_values = jnp.take(values, upper_node, axis=axis)
    bcast_shape = [1] * values.ndim
    bcast_shape[axis] = fine_count
    weight = weight.reshape(bcast_shape)
    return (1.0 - weight) * lower_values + weight * upper_values


def slot_match(mine, theirs):
    return (mine[..., :, None] == theirs[..., None, :]).astype(jnp.float32)


def neighbour_sum(fields, grain_ids):
    blocks = fields.reshape(Q, N_SLAB, CX, N_COL, CY, FINE_CELLS_HEIGHT)
    prev_slab = slot_match(grain_ids, jnp.roll(grain_ids, 1, axis=0))
    next_slab = slot_match(grain_ids, jnp.roll(grain_ids, -1, axis=0))
    prev_col = slot_match(grain_ids, jnp.roll(grain_ids, 1, axis=1))
    next_col = slot_match(grain_ids, jnp.roll(grain_ids, -1, axis=1))
    top_faces = blocks[:, :, CX - 1]
    bottom_faces = blocks[:, :, 0]
    zero_slab = jnp.zeros_like(top_faces[:, :1])
    from_below = jnp.concatenate([zero_slab, top_faces[:, :-1]], axis=1)
    from_above = jnp.concatenate([bottom_faces[:, 1:], zero_slab], axis=1)
    below = jnp.einsum("scqr,rscyz->qscyz", prev_slab, from_below, precision=FULL_ACCURACY)
    above = jnp.einsum("scqr,rscyz->qscyz", next_slab, from_above, precision=FULL_ACCURACY)
    x_low = jnp.concatenate([below[:, :, None], blocks[:, :, :-1]], axis=2)
    x_high = jnp.concatenate([blocks[:, :, 1:], above[:, :, None]], axis=2)
    right_faces = blocks[:, :, :, :, CY - 1]
    left_faces = blocks[:, :, :, :, 0]
    zero_col = jnp.zeros_like(right_faces[:, :, :, :1])
    from_left = jnp.concatenate([zero_col, right_faces[:, :, :, :-1]], axis=3)
    from_right = jnp.concatenate([left_faces[:, :, :, 1:], zero_col], axis=3)
    lefts = jnp.einsum("scqr,rsxcz->qsxcz", prev_col, from_left, precision=FULL_ACCURACY)
    rights = jnp.einsum("scqr,rsxcz->qsxcz", next_col, from_right, precision=FULL_ACCURACY)
    y_low = jnp.concatenate([lefts[:, :, :, :, None], blocks[:, :, :, :, :-1]], axis=4)
    y_high = jnp.concatenate([blocks[:, :, :, :, 1:], rights[:, :, :, :, None]], axis=4)
    x_low = x_low.reshape(fields.shape)
    x_high = x_high.reshape(fields.shape)
    y_low = y_low.reshape(fields.shape)
    y_high = y_high.reshape(fields.shape)
    zero_plane = jnp.zeros((Q, FINE_CELLS_TRACK, FINE_CELLS_ACROSS, 1), jnp.float32)
    z_low = jnp.concatenate([zero_plane, fields[..., :-1]], axis=3)
    z_high = jnp.concatenate([fields[..., 1:], zero_plane], axis=3)
    return x_low + x_high + y_low + y_high + z_low + z_high


def rates(fields, laplace, grain_mobility, slot_energy):
    squares = jnp.sum(fields * fields, axis=0)
    force = (-fields + fields * fields * fields
             + 2.0 * COUPLING * fields * (squares - fields * fields)
             - laplace - slot_energy * fields * (1.0 - fields))
    return -grain_mobility * force


def reference(order_params, layer_mask, coarse_temp, coarse_rows, grain_ids, energy):
    block_ends = jnp.cumsum(coarse_rows).astype(jnp.int32)
    block_starts = (block_ends - coarse_rows).astype(jnp.int32)
    plane = jnp.arange(NXC, dtype=jnp.int32)
    owner = jnp.sum((block_ends[None, :] <= plane[:, None]).astype(jnp.int32), axis=1).astype(jnp.int32)
    row_index = (owner * CAPX + plane - block_starts[owner]).astype(jnp.int32)
    coarse_mesh = coarse_temp[row_index]
    thermal_profile = linear_resample_axis(coarse_mesh, 0, FINE_CELLS_TRACK)
    thermal_profile = linear_resample_axis(thermal_profile, 1, FINE_CELLS_ACROSS)
    thermal_profile = linear_resample_axis(thermal_profile, 2, FINE_CELLS_HEIGHT)
    grain_mobility = jnp.exp(2.0 * (thermal_profile - 1.0))
    deposited = layer_mask.astype(jnp.float32)
    mobility_sum = Q * jnp.sum(deposited * grain_mobility)
    energy_blocks = energy[grain_ids]
    slot_energy = jnp.broadcast_to(
        jnp.transpose(energy_blocks, (2, 0, 1))[:, :, None, :, None, None],
        (Q, N_SLAB, CX, N_COL, CY, FINE_CELLS_HEIGHT)).reshape(Q, FINE_CELLS_TRACK, FINE_CELLS_ACROSS, FINE_CELLS_HEIGHT)
    fields = order_params
    for step_index in range(STEPS):
        laplace = neighbour_sum(fields, grain_ids) - 6.0 * fields
        rate = rates(fields, laplace, grain_mobility, slot_energy)
        multiplier = jnp.sum(deposited * jnp.sum(rate, axis=0)) / mobility_sum
        fields = fields + TIME_STEP * deposited * (rate - grain_mobility * multiplier)
    return fields
```

```python
import functools

import jax
import jax.numpy as jnp
from jax import lax
from jax.experimental import pallas as pl
from jax.experimental.pallas import tpu as pltpu
from jax.sharding import PartitionSpec as P

Q = 16
G = 4
CX = 8
CY = 8
NZ = 256
CAP = 6
CYC = 4
NZC = 128
TIME_STEP = 0.05
EXACT = lax.Precision.HIGHEST
MESH = pl.DeviceIdType.MESH
F32 = jnp.float32
I32 = jnp.int32


def near(face):
    return 1 if face in (0, 2) else 0


def kernel(
    torus,
    rows_s,
    ids_s,
    energy_s,
    fields_hbm,
    mask_hbm,
    coarse_hbm,
    out_ref,
    raw,
    mask,
    cb,
    pb,
    u_ref,
    v_ref,
    bf,
    nbi,
    rm,
    ym,
    yf,
    rf,
    ya,
    ra,
    st,
    ys,
    rs,
    hy,
    y2,
    r2,
    ar_src,
    ar_rcv,
    e_s,
    perm_s,
    pos_s,
    local_sem,
    send_sem,
    recv_sem,
):
    nx, nzt, ny, nk = torus
    slabs, cols = nx * nzt, ny * nk
    s = lax.axis_index("slab")
    c = lax.axis_index("col")
    tx, tz = s // nzt, s % nzt
    ty, tk = c // nk, c % nk
    planes_all = slabs * (CX // 2)
    rows_all = cols * CYC

    local = [
        pltpu.make_async_copy(coarse_hbm, cb.at[pl.ds(4 * CAP, CAP)], local_sem.at[0]),
        pltpu.make_async_copy(mask_hbm, mask, local_sem.at[1]),
        pltpu.make_async_copy(fields_hbm, raw, local_sem.at[2]),
    ]
    for copy in local:
        copy.start()

    def halo_peer(ds, dc):
        return ((s + ds + slabs) % slabs, (c + dc + cols) % cols)

    def peer_1(dz, dk):
        return (tx * nzt + (tz + dz) % nzt, ty * nk + (tk + dk) % nk)

    def peer_2(dx, dy):
        return (((tx + dx) % nx) * nzt + tz, ((ty + dy) % ny) * nk + tk)

    halo_offsets = [(a, b) for a in (-1, 0, 1) for b in (-1, 0, 1) if (a, b) != (0, 0)]
    group_1 = [(a, b) for a in range(nzt) for b in range(nk) if (a, b) != (0, 0)]
    group_2 = [(a, b) for a in range(nx) for b in range(ny) if (a, b) != (0, 0)]
    group_1.sort(key=lambda o: -min(o[0], nzt - o[0]))
    group_2.sort(key=lambda o: -(min(o[0], nx - o[0]) + min(o[1], ny - o[1])))
    peers = [halo_peer(*o) for o in halo_offsets]
    peers += [peer_1(*o) for o in group_1] + [peer_2(*o) for o in group_2]
    barrier = pltpu.get_barrier_semaphore()
    for peer in peers:
        pl.semaphore_signal(barrier, inc=1, device_id=peer, device_id_type=MESH)

    face_offset = ((-1, 0), (1, 0), (0, -1), (0, 1))
    has_flag = (s > 0, s < slabs - 1, c > 0, c < cols - 1)
    has = [jnp.where(flag, 1.0, 0.0).astype(F32) for flag in has_flag]

    count = [0]

    def send(src, dst, peer):
        at = count[0]
        count[0] += 1
        copy = pltpu.make_async_remote_copy(
            src_ref=src,
            dst_ref=dst,
            send_sem=send_sem.at[at],
            recv_sem=recv_sem.at[at],
            device_id=peer,
            device_id_type=MESH,
        )
        copy.start()
        return copy

    own = [ids_s[s, c, q] for q in range(Q)]
    group = [jnp.int32(-1)] * Q
    for face, (ds, dc) in enumerate(face_offset):
        sn = jnp.clip(s + ds, 0, slabs - 1)
        cn = jnp.clip(c + dc, 0, cols - 1)

        def match(r, found, sn=sn, cn=cn, face=face):
            other = jnp.where(has_flag[face], ids_s[sn, cn, r], -1)
            return tuple(jnp.where(o == other, face, g) for o, g in zip(own, found))

        group = lax.fori_loop(0, Q, match, tuple(group))
    first_free = jnp.where(s == 0, 0, jnp.where(s == slabs - 1, 1, jnp.where(c == 0, 2, 3)))
    last_free = jnp.where(c == 0, 2, 3)
    key = []
    for q in range(Q):
        free_rank = jnp.int32(0)
        for p in range(Q):
            if p != q:
                free_rank += jnp.where((group[p] < 0) & (own[p] < own[q]), 1, 0)
        place = jnp.where(free_rank < G, first_free, last_free)
        key.append(jnp.where(group[q] < 0, place, group[q]) * 65536 + own[q])
    for q in range(Q):
        rank = jnp.int32(0)
        for p in range(Q):
            if p != q:
                rank += jnp.where(key[p] < key[q], 1, 0)
        pos_s[q] = rank
    for p in range(Q):
        slot = jnp.int32(0)
        for q in range(1, Q):
            slot = jnp.where(pos_s[q] == p, q, slot)
        perm_s[p] = slot
        e_s[p] = energy_s[ids_s[s, c, slot]]
    e_total = e_s[0]
    for p in range(1, Q):
        e_total += e_s[p]

    start_own = jnp.int32(0)
    for i in range(slabs):
        start_own += jnp.where(i < s, rows_s[i], 0)
    end_own = start_own + rows_s[s]
    start_prev = start_own - rows_s[jnp.maximum(s - 1, 0)]

    zero_slab = jnp.zeros((CY, NZ), F32)
    for q in range(Q):
        for ref in (u_ref, v_ref):
            if q // G != 0:
                ref[q, 0:8, :] = zero_slab
            if q // G != 1:
                ref[q, 72:80, :] = zero_slab

    sub = lax.broadcasted_iota(I32, (CY, NZ), 0)
    lane = lax.broadcasted_iota(I32, (CY, NZ), 1)

    def column(view, start):
        rows = jnp.broadcast_to(view[pl.ds(start, 1), :], (CX, NZ))
        for x in range(1, CX):
            rows = jnp.where(sub == x, view[pl.ds(start + CY * x, 1), :], rows)
        return rows

    out_row = lax.broadcasted_iota(I32, (128, 64), 0)
    in_row = lax.broadcasted_iota(I32, (128, 64), 1)
    high = out_row >> 3
    low = out_row & 7
    along = jnp.where(
        out_row < 64,
        high,
        jnp.where(out_row < 80, high - 10, jnp.where(out_row < 96, high - 2, low)),
    )
    across = jnp.where(
        out_row < 96, low, jnp.where(out_row < 112, high - 14, high - 6)
    )

    def node_weight(fine, node):
        twice = 2 * fine - 1
        lower = twice >> 2
        w = (twice - 4 * lower).astype(F32) * 0.25
        return jnp.where(node == lower + 2, 1.0 - w, jnp.where(node == lower + 3, w, 0.0))

    weight_xy = node_weight(along, in_row >> 3) * node_weight(across, in_row & 7)
    node_z = lax.broadcasted_iota(I32, (NZC, NZ), 0)
    fine_z = lax.broadcasted_iota(I32, (NZC, NZ), 1)
    lower_z = (2 * fine_z - 1) >> 2
    w_z = (2 * fine_z - 1 - 4 * lower_z).astype(F32) * 0.25
    weight_z = jnp.where(node_z == jnp.clip(lower_z, 0, NZC - 1), 1.0 - w_z, 0.0) + jnp.where(
        node_z == jnp.clip(lower_z + 1, 0, NZC - 1), w_z, 0.0
    )

    local[1].wait()
    for k in range(2):
        ym[0, 8 * k : 8 * k + 8, :] = column(mask, k)
        ym[1, 8 * k : 8 * k + 8, :] = column(mask, 6 + k)
    local[2].wait()
    for p in range(Q):
        u_ref[p, 8:72, :] = raw[perm_s[p]]
    for j in range(G):
        yf[0, j] = column(u_ref.at[2 * G + j], 8)
        yf[1, j] = column(u_ref.at[3 * G + j], 15)
    local[0].wait()

    pl.semaphore_wait(barrier, len(peers))

    first = []
    for ds, dc in halo_offsets:
        slot = (1 - dc) * 3 + (1 - ds)
        first.append(
            send(
                cb.at[pl.ds(4 * CAP, CAP)], cb.at[pl.ds(slot * CAP, CAP)], halo_peer(ds, dc)
            )
        )
    mask_src = (mask.at[pl.ds(0, 16)], mask.at[pl.ds(48, 16)], ym.at[0], ym.at[1])
    field_src = (
        u_ref.at[pl.ds(0, G), pl.ds(8, 8)],
        u_ref.at[pl.ds(G, G), pl.ds(64, 8)],
        yf.at[0],
        yf.at[1],
    )
    mask_copies = []
    field_copies = []
    for face in range(4):
        mask_copies.append(send(mask_src[face], rm.at[face ^ 1], halo_peer(*face_offset[face])))
    for face in range(4):
        field_copies.append(send(field_src[face], rf.at[face ^ 1], halo_peer(*face_offset[face])))

    for copy in first:
        copy.wait_recv()
    for i in range(8):
        plane = jnp.clip(s * (CX // 2) - 2 + i, 0, planes_all - 1)
        flat = jnp.where(
            plane < start_own,
            plane - start_prev,
            jnp.where(plane < end_own, CAP + plane - start_own, 2 * CAP + plane - end_own),
        )
        flat = jnp.clip(flat, 0, 3 * CAP - 1)
        mine = cb[3 * CAP + flat]
        left = cb[flat, CYC - 2 : CYC, :]
        right = cb[6 * CAP + flat, 0:2, :]
        pb[8 * i : 8 * i + 2, :] = jnp.where(c == 0, mine[0:1], left)
        pb[8 * i + 2 : 8 * i + 6, :] = mine
        pb[8 * i + 6 : 8 * i + 8, :] = jnp.where(c == cols - 1, mine[CYC - 1 : CYC], right)
    profile = jnp.dot(weight_xy, pb[...], precision=EXACT, preferred_element_type=F32)
    profile = jnp.dot(profile, weight_z, precision=EXACT, preferred_element_type=F32)
    scaled = TIME_STEP * jnp.exp(2.0 * (profile - 1.0))
    bf[0:64, :] = scaled[0:64] * mask[...].astype(F32)
    for copy in mask_copies:
        copy.wait_recv()
    for face in range(4):
        at = 64 + 16 * face
        bf[at : at + 16, :] = scaled[at : at + 16] * rm[face].astype(F32) * has[face]

    def near_b(face):
        at = 64 + 16 * face + 8 * near(face)
        return bf[at : at + 8, :]

    def sides(f, low_row, high_row):
        total = jnp.where(sub == 0, low_row, pltpu.roll(f, 1, 0))
        total += jnp.where(sub == CY - 1, high_row, pltpu.roll(f, CY - 1, 0))
        total += jnp.where(lane == 0, 0.0, pltpu.roll(f, 1, 1))
        total += jnp.where(lane == NZ - 1, 0.0, pltpu.roll(f, NZ - 1, 1))
        return total

    sum_b = zero_slab
    sum_b4 = zero_slab
    sum_bnb = zero_slab
    for x in range(CX):
        b = bf[8 * x : 8 * x + 8, :]
        around = sides(b, 0.0, 0.0)
        if x > 0:
            around += bf[8 * x - 8 : 8 * x, :]
        if x < CX - 1:
            around += bf[8 * x + 8 : 8 * x + 16, :]
        nbi[8 * x : 8 * x + 8, :] = around
        square = b * b
        sum_b += b
        sum_b4 += square * square
        sum_bnb += 16.0 * b * around
    face_b = (
        bf[0:8, :],
        bf[56:64, :],
        column(bf, 0),
        column(bf, 7),
    )
    for face in range(4):
        sum_bnb += 4.0 * face_b[face] * near_b(face)

    for copy in field_copies:
        copy.wait_recv()
    for j in range(G):
        u_ref[j, 0:8, :] = rf[0, j] * has[0]
        u_ref[G + j, 72:80, :] = rf[1, j] * has[1]
        hy[0, j] = rf[2, j] * has[2]
        hy[1, j] = rf[3, j] * has[3]

    def stencil(src, dst, shift, sums):
        def body(x, carry):
            r = pl.multiple_of(8 * x, 8)
            b = bf[pl.ds(r, 8), :]
            squares = zero_slab
            for q in range(Q):
                f = src[q, pl.ds(r + 8, 8), :]
                squares += f * f
            common = 5.0 + 3.0 * squares
            force_all = zero_slab
            t1 = zero_slab
            t2 = zero_slab
            t3 = zero_slab
            te = zero_slab
            te2 = zero_slab
            for q in range(Q):
                e = e_s[q]
                f = src[q, pl.ds(r + 8, 8), :]
                low_row = hy[0, q - 2 * G, pl.ds(x, 1), :] if q // G == 2 else 0.0
                high_row = hy[1, q - 3 * G, pl.ds(x, 1), :] if q // G == 3 else 0.0
                around = src[q, pl.ds(r, 8), :] + src[q, pl.ds(r + 16, 8), :]
                around += sides(f, low_row, high_row)
                force = f * ((common - e) + f * (e - 2.0 * f)) - around
                if sums:
                    a = f - b * force
                    force_all += force
                    square = a * a
                    ea = e * a
                    t1 += a
                    t2 += square
                    t3 += square * a
                    te += ea
                    te2 += ea * a
                else:
                    a = f - b * (force + shift)
                dst[q, pl.ds(r + 8, 8), :] = a
            if not sums:
                return carry
            st[0, pl.ds(r, 8), :] = t2
            st[1, pl.ds(r, 8), :] = t1
            total, k0, k1, k2 = carry
            b2 = b * b
            total += b * force_all
            k0 += b * (t1 * (5.0 + 3.0 * t2) - te + te2 - 2.0 * t3) - t1 * nbi[pl.ds(r, 8), :]
            k1 += b2 * (e_total - 80.0 - 42.0 * t2 - 6.0 * t1 * t1 - 2.0 * te)
            k2 += b2 * b * (138.0 * t1 + e_total)
            return total, k0, k1, k2

        start = (zero_slab,) * 4 if sums else 0
        return lax.fori_loop(0, CX, body, start)

    def face_sum(k0):
        for j in range(G):
            k0 -= v_ref[j, 8:16, :] * near_b(0)
            k0 -= v_ref[G + j, 64:72, :] * near_b(1)
            k0 -= column(v_ref.at[2 * G + j], 8) * near_b(2)
            k0 -= column(v_ref.at[3 * G + j], 15) * near_b(3)
        return k0

    lane_1 = lax.broadcasted_iota(I32, (1, 128), 1)

    def put_row(at, parts):
        row = jnp.zeros((1, 128), F32)
        for k, part in enumerate(parts):
            value = jnp.sum(jnp.sum(part, axis=0, keepdims=True), axis=1, keepdims=True)
            row += jnp.where(lane_1 == k, value, 0.0)
        ar_src[at] = row

    def spread(at, offsets, peer_of):
        return [
            send(ar_src.at[at], ar_rcv.at[at, k], peer_of(*offset))
            for k, offset in enumerate(offsets)
        ]

    def gathered(at, copies):
        for copy in copies:
            copy.wait_recv()
        row = ar_src[at]
        for k in range(len(copies)):
            row += ar_rcv[at, k]
        return row

    def two_multipliers(row):
        got = [
            jnp.sum(jnp.where(lane_1 == k, row, 0.0), axis=1, keepdims=True) for k in range(6)
        ]
        inverse = -1.0 / (16.0 * got[0])
        m_a = got[1] * inverse
        m_b = (got[2] + m_a * (got[3] + m_a * (got[4] + m_a * got[5]))) * inverse
        return jnp.broadcast_to(m_a, (CY, NZ)), jnp.broadcast_to(m_b, (CY, NZ))

    def all_sums(at, parts, between):
        total, k0, k1, k2 = parts
        put_row(at, (sum_b, total, face_sum(k0), k1 + sum_bnb, k2, -736.0 * sum_b4))
        copies = spread(at, group_1, peer_1)
        extra = between()
        ar_src[at + 1] = gathered(at, copies)
        more = spread(at + 1, group_2, peer_2)
        result = two_multipliers(gathered(at + 1, more))
        return result, extra, copies + more

    parts = stencil(u_ref, v_ref, None, True)

    def send_deep():
        copies = []
        for j in range(G):
            for k in range(2):
                ya[0, j, 8 * k : 8 * k + 8, :] = column(v_ref.at[2 * G + j], 8 + k)
                ya[1, j, 8 * k : 8 * k + 8, :] = column(v_ref.at[3 * G + j], 14 + k)
        for k in range(2):
            ys[0, k] = column(st.at[k], 0)
            ys[1, k] = column(st.at[k], 7)
        deep = (
            v_ref.at[pl.ds(0, G), pl.ds(8, 16)],
            v_ref.at[pl.ds(G, G), pl.ds(56, 16)],
            ya.at[0],
            ya.at[1],
        )
        flat = (st.at[:, pl.ds(0, 8)], st.at[:, pl.ds(56, 8)], ys.at[0], ys.at[1])
        for face in range(4):
            peer = halo_peer(*face_offset[face])
            copies.append(send(deep[face], ra.at[face ^ 1], peer))
            copies.append(send(flat[face], rs.at[face ^ 1], peer))
        return copies

    (m0, m1), deep_copies, sent_1 = all_sums(0, parts, send_deep)

    for copy in field_copies:
        copy.wait_send()
    for copy in deep_copies:
        copy.wait()

    def settle(m):
        def body(x, carry):
            r = pl.multiple_of(8 * x, 8)
            mb = m * bf[pl.ds(r, 8), :]
            for q in range(Q):
                v_ref[q, pl.ds(r + 8, 8), :] = v_ref[q, pl.ds(r + 8, 8), :] - mb
            return carry

        lax.fori_loop(0, CX, body, 0)

    settle(m0)
    for face in range(4):
        at = 64 + 16 * face
        for k in range(2):
            mb = m0 * bf[at + 8 * k : at + 8 * k + 8, :]
            for j in range(G):
                value = ra[face, j, 8 * k : 8 * k + 8, :] * has[face] - mb
                ra[face, j, 8 * k : 8 * k + 8, :] = value
                if k == near(face):
                    if face == 0:
                        v_ref[j, 0:8, :] = value
                    elif face == 1:
                        v_ref[G + j, 72:80, :] = value
                    else:
                        hy[face - 2, j] = value

    for face in range(4):
        b = near_b(face)
        mb = m0 * b
        squares = rs[face, 0] - 2.0 * mb * rs[face, 1] + 16.0 * mb * mb
        common = 5.0 + 3.0 * squares
        here, beyond = 8 * near(face), 8 * (1 - near(face))
        for j in range(G):
            q = face * G + j
            e = e_s[q]
            f = ra[face, j, here : here + 8, :]
            if face == 0:
                inner = v_ref[q, 8:16, :]
            elif face == 1:
                inner = v_ref[q, 64:72, :]
            elif face == 2:
                inner = column(v_ref.at[q], 8)
            else:
                inner = column(v_ref.at[q], 15)
            around = ra[face, j, beyond : beyond + 8, :] + inner + sides(f, 0.0, 0.0)
            force = f * ((common - e) + f * (e - 2.0 * f)) - around
            value = f - b * (force + m1)
            if face == 0:
                u_ref[j, 0:8, :] = value
            elif face == 1:
                u_ref[G + j, 72:80, :] = value
            else:
                y2[face - 2, j] = value
    stencil(v_ref, u_ref, m1, False)
    for j in range(G):
        hy[0, j] = y2[0, j]
        hy[1, j] = y2[1, j]

    parts = stencil(u_ref, v_ref, None, True)

    def send_shallow():
        for j in range(G):
            y2[0, j] = column(v_ref.at[2 * G + j], 8)
            y2[1, j] = column(v_ref.at[3 * G + j], 15)
        source = (
            v_ref.at[pl.ds(0, G), pl.ds(8, 8)],
            v_ref.at[pl.ds(G, G), pl.ds(64, 8)],
            y2.at[0],
            y2.at[1],
        )
        return [
            send(source[face], r2.at[face ^ 1], halo_peer(*face_offset[face]))
            for face in range(4)
        ]

    (m2, m3), shallow_copies, sent_2 = all_sums(2, parts, send_shallow)
    for copy in shallow_copies:
        copy.wait()
    settle(m2)
    mb = [m2 * near_b(face) for face in range(4)]
    for j in range(G):
        v_ref[j, 0:8, :] = r2[0, j] * has[0] - mb[0]
        v_ref[G + j, 72:80, :] = r2[1, j] * has[1] - mb[1]
        hy[0, j] = r2[2, j] * has[2] - mb[2]
        hy[1, j] = r2[3, j] * has[3] - mb[3]
    stencil(v_ref, u_ref, m3, False)
    for q in range(Q):
        out_ref[q] = u_ref[pos_s[q], 8:72, :]
    for copy in first + mask_copies + sent_1 + sent_2:
        copy.wait_send()


def per_device(torus, order_params, layer_mask, coarse_temp, coarse_rows, grain_ids, energy):
    any_space = pl.BlockSpec(memory_space=pl.ANY)
    smem = pl.BlockSpec(memory_space=pltpu.SMEM)
    vmem = pl.BlockSpec(memory_space=pltpu.VMEM)
    nx, nzt, ny, nk = torus
    copies = 16 + 8 + 4 + 2 * (nzt * nk - 1 + nx * ny - 1)
    slots = max(nzt * nk, nx * ny)
    rows = CX * CY
    out = pl.pallas_call(
        functools.partial(kernel, torus),
        out_shape=jax.ShapeDtypeStruct((Q, rows, NZ), F32),
        in_specs=[smem] * 3 + [any_space] * 3,
        out_specs=vmem,
        scratch_shapes=[
            pltpu.VMEM((Q, rows, NZ), F32),
            pltpu.VMEM((rows, NZ), I32),
            pltpu.VMEM((9 * CAP, CYC, NZC), F32),
            pltpu.VMEM((64, NZC), F32),
            pltpu.VMEM((Q, rows + 16, NZ), F32),
            pltpu.VMEM((Q, rows + 16, NZ), F32),
            pltpu.VMEM((128, NZ), F32),
            pltpu.VMEM((rows, NZ), F32),
            pltpu.VMEM((4, 16, NZ), I32),
            pltpu.VMEM((2, 16, NZ), I32),
            pltpu.VMEM((2, G, 8, NZ), F32),
            pltpu.VMEM((4, G, 8, NZ), F32),
            pltpu.VMEM((2, G, 16, NZ), F32),
            pltpu.VMEM((4, G, 16, NZ), F32),
            pltpu.VMEM((2, rows, NZ), F32),
            pltpu.VMEM((2, 2, 8, NZ), F32),
            pltpu.VMEM((4, 2, 8, NZ), F32),
            pltpu.VMEM((2, G, 8, NZ), F32),
            pltpu.VMEM((2, G, 8, NZ), F32),
            pltpu.VMEM((4, G, 8, NZ), F32),
            pltpu.VMEM((4, 1, 128), F32),
            pltpu.VMEM((4, slots, 1, 128), F32),
            pltpu.SMEM((Q,), F32),
            pltpu.SMEM((Q,), I32),
            pltpu.SMEM((Q,), I32),
            pltpu.SemaphoreType.DMA((3,)),
            pltpu.SemaphoreType.DMA((copies,)),
            pltpu.SemaphoreType.DMA((copies,)),
        ],
        compiler_params=pltpu.CompilerParams(collective_id=0, has_side_effects=True),
    )(
        coarse_rows,
        grain_ids,
        energy,
        order_params.reshape(Q, rows, NZ),
        layer_mask.reshape(rows, NZ),
        coarse_temp,
    )
    return out.reshape(Q, CX, CY, NZ)


def solution(mesh, torus=(4, 8, 4, 2)):
    placed = (
        P(None, "slab", "col", None),
        P("slab", "col", None),
        P("slab", "col", None),
        P(),
        P(),
        P(),
    )
    return jax.shard_map(
        functools.partial(per_device, torus),
        mesh=mesh,
        in_specs=placed,
        out_specs=P(None, "slab", "col", None),
        check_vma=False,
    )
```

```python
import functools

import jax
import jax.numpy as jnp
from jax import lax
from jax.experimental import pallas as pl
from jax.experimental.pallas import tpu as pltpu
from jax.sharding import PartitionSpec as P

Q = 16
G = 4
CX = 8
CY = 8
NZ = 256
CAP = 6
CYC = 4
NZC = 128
TIME_STEP = 0.05
EXACT = lax.Precision.HIGHEST
MESH = pl.DeviceIdType.MESH
F32 = jnp.float32
I32 = jnp.int32


def near(face):
    return 1 if face in (0, 2) else 0


def wait_for(ref, sem):
    pltpu.make_async_copy(ref, ref, sem).wait()


def kernel(
    torus,
    rows_hbm,
    ids_hbm,
    energy_hbm,
    fields_hbm,
    mask_hbm,
    coarse_hbm,
    out_ref,
    pos_s,
    raw,
    mask,
    cb,
    cl,
    cr,
    pb,
    u_ref,
    v_ref,
    bf,
    nbi,
    nbg,
    rm,
    ym,
    yf,
    rf,
    ya,
    ra,
    st,
    ys,
    rs,
    sq,
    hy,
    ah,
    nh,
    nbh,
    y2,
    r2,
    ar_src,
    ar_1a,
    ar_1b,
    ar_2a,
    ar_2b,
    rows_s,
    ids_s,
    energy_s,
    e_s,
    perm_s,
    local_sem,
    send_sem,
    recv_sem,
):
    nx, nzt, ny, nk = torus
    slabs, cols = nx * nzt, ny * nk
    s = lax.axis_index("slab")
    c = lax.axis_index("col")
    tx, tz = s // nzt, s % nzt
    ty, tk = c // nk, c % nk
    planes_all = slabs * (CX // 2)
    col_low, col_high = jnp.maximum(c - 1, 0), jnp.minimum(c + 1, cols - 1)

    local = [
        pltpu.make_async_copy(ids_hbm.at[c], ids_s.at[0], local_sem.at[0]),
        pltpu.make_async_copy(ids_hbm.at[col_low], ids_s.at[1], local_sem.at[1]),
        pltpu.make_async_copy(ids_hbm.at[col_high], ids_s.at[2], local_sem.at[2]),
        pltpu.make_async_copy(energy_hbm, energy_s, local_sem.at[3]),
        pltpu.make_async_copy(rows_hbm, rows_s, local_sem.at[4]),
        pltpu.make_async_copy(fields_hbm, raw, local_sem.at[5]),
        pltpu.make_async_copy(mask_hbm, mask, local_sem.at[6]),
        pltpu.make_async_copy(coarse_hbm, cb.at[pl.ds(CAP, CAP)], local_sem.at[7]),
    ]
    for copy in local:
        copy.start()

    def halo_peer(ds, dc):
        return ((s + ds + slabs) % slabs, (c + dc + cols) % cols)

    def torus_peer(dx, dy, dz, dk):
        qx = (tx + dx) % nx if dx else tx
        qy = (ty + dy) % ny if dy else ty
        qz = (tz + dz) % nzt if dz else tz
        qk = (tk + dk) % nk if dk else tk
        return (qx * nzt + qz, qy * nk + qk)

    def far(offset):
        return -sum(min(d, n - d) for d, n in zip(offset, (nx, ny, nzt, nk)))

    def offsets(sx, sy, sz, sk):
        every = [
            (a, b, d, e)
            for a in range(sx)
            for b in range(sy)
            for d in range(sz)
            for e in range(sk)
            if (a, b, d, e) != (0, 0, 0, 0)
        ]
        return sorted(every, key=far)

    halo_offsets = [(a, b) for a in (-1, 0, 1) for b in (-1, 0, 1) if (a, b) != (0, 0)]
    group_zk = offsets(1, 1, nzt, nk)
    group_xy = offsets(nx, ny, 1, 1)
    group_k = offsets(1, 1, 1, nk)
    group_xyz = offsets(nx, ny, nzt, 1)
    peers = [halo_peer(*o) for o in halo_offsets]
    peers += [torus_peer(*o) for o in group_zk + group_xy]
    barrier = pltpu.get_barrier_semaphore()
    for peer in peers:
        pl.semaphore_signal(barrier, inc=1, device_id=peer, device_id_type=MESH)

    face_offset = ((-1, 0), (1, 0), (0, -1), (0, 1))
    has_flag = (s > 0, s < slabs - 1, c > 0, c < cols - 1)
    has = [jnp.where(flag, 1.0, 0.0).astype(F32) for flag in has_flag]

    def send(src, dst, peer, sem):
        pltpu.make_async_remote_copy(
            src_ref=src,
            dst_ref=dst,
            send_sem=send_sem.at[sem],
            recv_sem=recv_sem.at[sem],
            device_id=peer,
            device_id_type=MESH,
        ).start()

    sub = lax.broadcasted_iota(I32, (CY, NZ), 0)
    lane = lax.broadcasted_iota(I32, (CY, NZ), 1)
    zero_slab = jnp.zeros((CY, NZ), F32)

    def column(view, start):
        rows = jnp.broadcast_to(view[pl.ds(start, 1), :], (CX, NZ))
        for x in range(1, CX):
            rows = jnp.where(sub == x, view[pl.ds(start + CY * x, 1), :], rows)
        return rows

    for copy in local[:3]:
        copy.wait()
    own = [ids_s[0, q, s] for q in range(Q)]
    group = [jnp.int32(-1)] * Q
    for face, (ds, dc) in enumerate(face_offset):
        sn = jnp.clip(s + ds, 0, slabs - 1)
        which = (0, 0, 1, 2)[face]

        def match(r, found, sn=sn, which=which, face=face):
            other = jnp.where(has_flag[face], ids_s[which, r, sn], -1)
            return tuple(jnp.where(o == other, face, g) for o, g in zip(own, found))

        group = lax.fori_loop(0, Q, match, tuple(group))
    first_free = jnp.where(s == 0, 0, jnp.where(s == slabs - 1, 1, jnp.where(c == 0, 2, 3)))
    last_free = jnp.where(c == 0, 2, 3)
    key = []
    for q in range(Q):
        free_rank = jnp.int32(0)
        for p in range(Q):
            if p != q:
                free_rank += jnp.where((group[p] < 0) & (own[p] < own[q]), 1, 0)
        place = jnp.where(free_rank < G, first_free, last_free)
        key.append(jnp.where(group[q] < 0, place, group[q]) * 65536 + own[q])
    for q in range(Q):
        rank = jnp.int32(0)
        for p in range(Q):
            if p != q:
                rank += jnp.where(key[p] < key[q], 1, 0)
        pos_s[q] = rank
    for p in range(Q):
        slot = jnp.int32(0)
        for q in range(1, Q):
            slot = jnp.where(pos_s[q] == p, q, slot)
        perm_s[p] = slot

    local[5].wait()
    for p in range(Q):
        u_ref[p, 8:72, :] = raw[perm_s[p]]
    for j in range(G):
        yf[0, j] = column(u_ref.at[2 * G + j], 8)
        yf[1, j] = column(u_ref.at[3 * G + j], 15)
    local[6].wait()
    for k in range(2):
        ym[0, 8 * k : 8 * k + 8, :] = column(mask, k)
        ym[1, 8 * k : 8 * k + 8, :] = column(mask, 6 + k)

    pl.semaphore_wait(barrier, len(peers))

    for ds, dc in halo_offsets:
        at = pl.ds((1 - ds) * CAP, CAP)
        if dc == 0:
            send(coarse_hbm, cb.at[at], halo_peer(ds, dc), 0)
        else:
            send(coarse_hbm, (cl if dc > 0 else cr).at[at], halo_peer(ds, dc), 1 if dc > 0 else 2)
    field_src = (
        u_ref.at[pl.ds(0, G), pl.ds(8, 8)],
        u_ref.at[pl.ds(G, G), pl.ds(64, 8)],
        yf.at[0],
        yf.at[1],
    )
    mask_src = (mask.at[pl.ds(0, 16)], mask.at[pl.ds(48, 16)], ym.at[0], ym.at[1])
    for face in range(4):
        send(field_src[face], rf.at[face ^ 1], halo_peer(*face_offset[face]), 3)
    for face in range(4):
        send(mask_src[face], rm.at[face ^ 1], halo_peer(*face_offset[face]), 4)

    for q in range(Q):
        for ref in (u_ref, v_ref):
            ref[q, 0:8, :] = zero_slab
            ref[q, 72:80, :] = zero_slab
    local[3].wait()
    for p in range(Q):
        e_s[p] = energy_s[ids_s[0, perm_s[p], s]]
    e_total = e_s[0]
    for p in range(1, Q):
        e_total += e_s[p]
    local[4].wait()
    start_own = jnp.int32(0)
    for i in range(slabs):
        start_own += jnp.where(i < s, rows_s[i], 0)
    end_own = start_own + rows_s[s]
    start_prev = start_own - rows_s[jnp.maximum(s - 1, 0)]

    def sides(f, low_row, high_row):
        total = jnp.where(sub == 0, low_row, pltpu.roll(f, 1, 0))
        total += jnp.where(sub == CY - 1, high_row, pltpu.roll(f, CY - 1, 0))
        total += jnp.where(lane == 0, 0.0, pltpu.roll(f, 1, 1))
        total += jnp.where(lane == NZ - 1, 0.0, pltpu.roll(f, NZ - 1, 1))
        return total

    def inside(src, squares):
        def body(x, carry):
            r = pl.multiple_of(8 * x, 8)
            total = zero_slab
            for q in range(Q):
                f = src[q, pl.ds(r + 8, 8), :]
                around = src[q, pl.ds(r, 8), :] + src[q, pl.ds(r + 16, 8), :]
                raw[q, pl.ds(r, 8), :] = around + sides(f, 0.0, 0.0)
                if squares:
                    total += f * f
            if squares:
                sq[pl.ds(r, 8), :] = total
            return carry

        lax.fori_loop(0, CX, body, 0)

    def add_faces(halo):
        for j in range(G):
            raw[j, 0:8, :] = raw[j, 0:8, :] + halo(0, j)
            raw[G + j, 56:64, :] = raw[G + j, 56:64, :] + halo(1, j)
            low, high = halo(2, j), halo(3, j)
            for x in range(CX):
                at = slice(8 * x, 8 * x + 8)
                row = jnp.where(sub == 0, low[x : x + 1, :], 0.0)
                raw[2 * G + j, at, :] = raw[2 * G + j, at, :] + row
                row = jnp.where(sub == CY - 1, high[x : x + 1, :], 0.0)
                raw[3 * G + j, at, :] = raw[3 * G + j, at, :] + row

    inside(u_ref, True)

    out_row = lax.broadcasted_iota(I32, (128, 64), 0)
    in_row = lax.broadcasted_iota(I32, (128, 64), 1)
    high = out_row >> 3
    low = out_row & 7
    along = jnp.where(
        out_row < 64,
        high,
        jnp.where(out_row < 80, high - 10, jnp.where(out_row < 96, high - 2, low)),
    )
    across = jnp.where(out_row < 96, low, jnp.where(out_row < 112, high - 14, high - 6))

    def node_weight(fine, node):
        twice = 2 * fine - 1
        lower = twice >> 2
        w = (twice - 4 * lower).astype(F32) * 0.25
        return jnp.where(node == lower + 2, 1.0 - w, jnp.where(node == lower + 3, w, 0.0))

    weight_xy = node_weight(along, in_row >> 3) * node_weight(across, in_row & 7)
    node_z = lax.broadcasted_iota(I32, (NZC, NZ), 0)
    fine_z = lax.broadcasted_iota(I32, (NZC, NZ), 1)
    lower_z = (2 * fine_z - 1) >> 2
    w_z = (2 * fine_z - 1 - 4 * lower_z).astype(F32) * 0.25
    weight_z = jnp.where(node_z == jnp.clip(lower_z, 0, NZC - 1), 1.0 - w_z, 0.0) + jnp.where(
        node_z == jnp.clip(lower_z + 1, 0, NZC - 1), w_z, 0.0
    )

    local[7].wait()
    wait_for(cb.at[pl.ds(0, 2 * CAP)], recv_sem.at[0])
    wait_for(cl, recv_sem.at[1])
    wait_for(cr, recv_sem.at[2])
    for i in range(8):
        plane = jnp.clip(s * (CX // 2) - 2 + i, 0, planes_all - 1)
        flat = jnp.where(
            plane < start_own,
            plane - start_prev,
            jnp.where(plane < end_own, CAP + plane - start_own, 2 * CAP + plane - end_own),
        )
        flat = jnp.clip(flat, 0, 3 * CAP - 1)
        mine = cb[flat]
        left = cl[flat, CYC - 2 : CYC, :]
        right = cr[flat, 0:2, :]
        pb[8 * i : 8 * i + 2, :] = jnp.where(c == 0, mine[0:1], left)
        pb[8 * i + 2 : 8 * i + 6, :] = mine
        pb[8 * i + 6 : 8 * i + 8, :] = jnp.where(c == cols - 1, mine[CYC - 1 : CYC], right)
    profile = jnp.dot(weight_xy, pb[...], precision=EXACT, preferred_element_type=F32)
    profile = jnp.dot(profile, weight_z, precision=EXACT, preferred_element_type=F32)
    scaled = TIME_STEP * jnp.exp(2.0 * (profile - 1.0))
    bf[0:64, :] = scaled[0:64] * mask[...].astype(F32)
    bf[64:128, :] = scaled[64:128]

    wait_for(rf, recv_sem.at[3])
    add_faces(lambda face, j: rf[face, j] * has[face])

    def near_b(face):
        at = 64 + 16 * face + 8 * near(face)
        return bf[at : at + 8, :]

    def react(src, dst, offset, shift, sums):
        def body(x, carry):
            r = pl.multiple_of(8 * x, 8)
            b = bf[pl.ds(r, 8), :]
            if shift is None:
                squares = sq[pl.ds(r, 8), :]
            else:
                m, extra = shift
                mb = m * b
                squares = st[0, pl.ds(r, 8), :] + mb * (16.0 * mb - 2.0 * st[1, pl.ds(r, 8), :])
                base = [extra + m * nbg[g, pl.ds(r, 8), :] for g in range(4)]
            common = 5.0 + 3.0 * squares
            acc = [zero_slab] * 6
            for q in range(Q):
                e = e_s[q]
                f = src[q, pl.ds(r + 8, 8), :]
                if shift is not None:
                    f = f - mb
                force = f * ((common - e) + f * (e - 2.0 * f))
                if sums and shift is None and src is not v_ref and offset is not None:
                    around = raw[q, pl.ds(r, 8), :]
                elif shift is None:
                    low_row = hy[0, q - 2 * G, pl.ds(x, 1), :] if q // G == 2 else 0.0
                    high_row = hy[1, q - 3 * G, pl.ds(x, 1), :] if q // G == 3 else 0.0
                    around = src[q, pl.ds(r, 8), :] + src[q, pl.ds(r + 16, 8), :]
                    around += sides(f, low_row, high_row)
                else:
                    around = raw[q, pl.ds(r, 8), :] - base[q // G]
                force = force - around
                a = f - b * force
                if sums:
                    square = a * a
                    ea = e * a
                    step = (force, a, square, square * a, ea, ea * a)
                    acc = [total + value for total, value in zip(acc, step)]
                elif dst is u_ref:
                    acc[0] += a * a
                dst[q, pl.ds(r + (offset or 8 if dst is not out_ref else 0), 8), :] = a
            if not sums:
                if dst is u_ref:
                    sq[pl.ds(r, 8), :] = acc[0]
                return carry
            force_all, t1, t2, t3, te, te2 = acc
            st[0, pl.ds(r, 8), :] = t2
            st[1, pl.ds(r, 8), :] = t1
            total, k0, k1, k2 = carry
            b2 = b * b
            total += b * force_all
            k0 += b * (t1 * (5.0 + 3.0 * t2) - te + te2 - 2.0 * t3) - t1 * nbi[pl.ds(r, 8), :]
            k1 += b2 * (e_total - 80.0 - 42.0 * t2 - 6.0 * t1 * t1 - 2.0 * te)
            k2 += b2 * b * (138.0 * t1 + e_total)
            return total, k0, k1, k2

        start = (zero_slab,) * 4 if sums else 0
        return lax.fori_loop(0, CX, body, start)

    sum_b = zero_slab
    sum_b4 = zero_slab
    sum_bnb = zero_slab
    for x in range(CX):
        b = bf[8 * x : 8 * x + 8, :]
        around = sides(b, 0.0, 0.0)
        if x > 0:
            around += bf[8 * x - 8 : 8 * x, :]
        if x < CX - 1:
            around += bf[8 * x + 8 : 8 * x + 16, :]
        nbi[8 * x : 8 * x + 8, :] = around
        square = b * b
        sum_b += b
        sum_b4 += square * square
        sum_bnb += 16.0 * b * around

    parts = react(u_ref, v_ref, 8, None, True)

    wait_for(rm, recv_sem.at[4])
    for face in range(4):
        at = 64 + 16 * face
        bf[at : at + 16, :] = bf[at : at + 16, :] * rm[face].astype(F32) * has[face]
    face_b = (bf[0:8, :], bf[56:64, :], column(bf, 0), column(bf, 7))
    for face in range(4):
        sum_bnb += 4.0 * face_b[face] * near_b(face)

    for j in range(G):
        for k in range(2):
            ya[0, j, 8 * k : 8 * k + 8, :] = column(v_ref.at[2 * G + j], 8 + k)
            ya[1, j, 8 * k : 8 * k + 8, :] = column(v_ref.at[3 * G + j], 14 + k)

    lane_1 = lax.broadcasted_iota(I32, (1, 128), 1)

    def put_row(at, parts, faces):
        total, k0, k1, k2 = parts
        for face in range(4):
            layer = faces[face][0]
            for j in range(1, G):
                layer = layer + faces[face][j]
            k0 -= layer * near_b(face)
        row = jnp.zeros((1, 128), F32)
        every = (sum_b, total, k0, k1 + sum_bnb, k2, -736.0 * sum_b4)
        for k, part in enumerate(every):
            value = jnp.sum(jnp.sum(part, axis=0, keepdims=True), axis=1, keepdims=True)
            row += jnp.where(lane_1 == k, value, 0.0)
        ar_src[at] = row

    def spread(at, group, landing, sem):
        for k, offset in enumerate(group):
            send(ar_src.at[at], landing.at[k], torus_peer(*offset), sem)

    def gathered(at, landing, sem):
        wait_for(landing, recv_sem.at[sem])
        return ar_src[at] + jnp.sum(landing[...], axis=0)

    def two_multipliers(row):
        got = [
            jnp.sum(jnp.where(lane_1 == k, row, 0.0), axis=1, keepdims=True) for k in range(6)
        ]
        inverse = -1.0 / (16.0 * got[0])
        m_a = got[1] * inverse
        m_b = (got[2] + m_a * (got[3] + m_a * (got[4] + m_a * got[5]))) * inverse
        return jnp.broadcast_to(m_a, (CY, NZ)), jnp.broadcast_to(m_b, (CY, NZ))

    put_row(
        0,
        parts,
        (
            [v_ref[j, 8:16, :] for j in range(G)],
            [v_ref[G + j, 64:72, :] for j in range(G)],
            [ya[0, j, 0:8, :] for j in range(G)],
            [ya[1, j, 8:16, :] for j in range(G)],
        ),
    )
    spread(0, group_zk, ar_1a, 5)

    for k in range(2):
        ys[0, k] = column(st.at[k], 0)
        ys[1, k] = column(st.at[k], 7)
    deep = (
        v_ref.at[pl.ds(0, G), pl.ds(8, 16)],
        v_ref.at[pl.ds(G, G), pl.ds(56, 16)],
        ya.at[0],
        ya.at[1],
    )
    flat = (st.at[:, pl.ds(0, 8)], st.at[:, pl.ds(56, 8)], ys.at[0], ys.at[1])
    for face in range(4):
        peer = halo_peer(*face_offset[face])
        send(deep[face], ra.at[face ^ 1], peer, 6)
        send(flat[face], rs.at[face ^ 1], peer, 7)
    inside(v_ref, False)
    for x in range(CX):
        at = slice(8 * x, 8 * x + 8)
        here = nbi[at, :]
        nbg[0, at, :] = here + near_b(0) if x == 0 else here
        nbg[1, at, :] = here + near_b(1) if x == CX - 1 else here
        nbg[2, at, :] = here + jnp.where(sub == 0, near_b(2)[x : x + 1, :], 0.0)
        nbg[3, at, :] = here + jnp.where(sub == CY - 1, near_b(3)[x : x + 1, :], 0.0)

    ar_src[1] = gathered(0, ar_1a, 5)
    spread(1, group_xy, ar_1b, 8)

    wait_for(ra, recv_sem.at[6])
    wait_for(rs, recv_sem.at[7])
    for face in range(4):
        here, beyond = 8 * near(face), 8 * (1 - near(face))
        at = 64 + 16 * face
        b = near_b(face)
        nbh[face] = bf[at + beyond : at + beyond + 8, :] + face_b[face] + sides(b, 0.0, 0.0)
        for j in range(G):
            value = ra[face, j, here : here + 8, :] * has[face]
            ah[face, j] = value
            if face == 0:
                inner = v_ref[j, 8:16, :]
            elif face == 1:
                inner = v_ref[G + j, 64:72, :]
            elif face == 2:
                inner = ya[0, j, 0:8, :]
            else:
                inner = ya[1, j, 8:16, :]
            outer = ra[face, j, beyond : beyond + 8, :]
            nh[face, j] = outer + inner + sides(value, 0.0, 0.0)
    add_faces(lambda face, j: ah[face, j])

    m0, m1 = two_multipliers(gathered(1, ar_1b, 8))

    wait_for(rf, send_sem.at[3])
    for face in range(4):
        b = near_b(face)
        mb = m0 * b
        squares = rs[face, 0] + mb * (16.0 * mb - 2.0 * rs[face, 1])
        common = 5.0 + 3.0 * squares
        base = m1 + m0 * nbh[face]
        for j in range(G):
            e = e_s[face * G + j]
            f = ah[face, j] - mb
            force = f * ((common - e) + f * (e - 2.0 * f)) - (nh[face, j] - base)
            value = f - b * force
            if face == 0:
                u_ref[j, 0:8, :] = value
            elif face == 1:
                u_ref[G + j, 72:80, :] = value
            else:
                hy[face - 2, j] = value
    react(v_ref, u_ref, 8, (m0, m1), False)

    wait_for(ra, send_sem.at[6])
    wait_for(rs, send_sem.at[7])
    parts = react(u_ref, v_ref, None, None, True)
    for j in range(G):
        y2[0, j] = column(v_ref.at[2 * G + j], 8)
        y2[1, j] = column(v_ref.at[3 * G + j], 15)
    put_row(
        2,
        parts,
        (
            [v_ref[j, 8:16, :] for j in range(G)],
            [v_ref[G + j, 64:72, :] for j in range(G)],
            [y2[0, j] for j in range(G)],
            [y2[1, j] for j in range(G)],
        ),
    )
    spread(2, group_k, ar_2a, 9)
    ar_src[3] = gathered(2, ar_2a, 9)
    spread(3, group_xyz, ar_2b, 10)
    shallow = (
        v_ref.at[pl.ds(0, G), pl.ds(8, 8)],
        v_ref.at[pl.ds(G, G), pl.ds(64, 8)],
        y2.at[0],
        y2.at[1],
    )
    for face in range(4):
        send(shallow[face], r2.at[face ^ 1], halo_peer(*face_offset[face]), 11)
    inside(v_ref, False)
    wait_for(r2, recv_sem.at[11])
    add_faces(lambda face, j: r2[face, j] * has[face])
    wait_for(cb.at[pl.ds(0, 2 * CAP)], send_sem.at[0])
    wait_for(cl, send_sem.at[1])
    wait_for(cr, send_sem.at[2])
    wait_for(rm, send_sem.at[4])
    wait_for(ar_1a, send_sem.at[5])
    wait_for(ar_1b, send_sem.at[8])
    wait_for(ar_2a, send_sem.at[9])
    wait_for(r2, send_sem.at[11])

    m2, m3 = two_multipliers(gathered(3, ar_2b, 10))
    react(v_ref, out_ref, 0, (m2, m3), False)
    wait_for(ar_2b, send_sem.at[10])


def write_out(pos_s, result, out_hbm, sem):
    copies = []
    for q in range(Q):
        copy = pltpu.make_async_copy(result.at[pos_s[q]], out_hbm.at[q], sem.at[q])
        copy.start()
        copies.append(copy)
    for copy in copies:
        copy.wait()


def per_device(torus, order_params, layer_mask, coarse_temp, coarse_rows, grain_ids, energy):
    any_space = pl.BlockSpec(memory_space=pl.ANY)
    smem = pl.BlockSpec(memory_space=pltpu.SMEM)
    vmem = pl.BlockSpec(memory_space=pltpu.VMEM)
    nx, nzt, ny, nk = torus
    slabs = nx * nzt
    rows = CX * CY

    def row_slots(count):
        return pltpu.VMEM((count, 1, 128), F32)

    result, pos = pl.pallas_call(
        functools.partial(kernel, torus),
        out_shape=(
            pltpu.VMEM((Q, rows, NZ), F32),
            jax.ShapeDtypeStruct((Q,), I32),
        ),
        in_specs=[any_space] * 6,
        out_specs=(vmem, smem),
        scratch_shapes=[
            pltpu.VMEM((Q, rows, NZ), F32),
            pltpu.VMEM((rows, NZ), I32),
            pltpu.VMEM((3 * CAP, CYC, NZC), F32),
            pltpu.VMEM((3 * CAP, CYC, NZC), F32),
            pltpu.VMEM((3 * CAP, CYC, NZC), F32),
            pltpu.VMEM((64, NZC), F32),
            pltpu.VMEM((Q, rows + 16, NZ), F32),
            pltpu.VMEM((Q, rows + 16, NZ), F32),
            pltpu.VMEM((128, NZ), F32),
            pltpu.VMEM((rows, NZ), F32),
            pltpu.VMEM((4, rows, NZ), F32),
            pltpu.VMEM((4, 16, NZ), I32),
            pltpu.VMEM((2, 16, NZ), I32),
            pltpu.VMEM((2, G, 8, NZ), F32),
            pltpu.VMEM((4, G, 8, NZ), F32),
            pltpu.VMEM((2, G, 16, NZ), F32),
            pltpu.VMEM((4, G, 16, NZ), F32),
            pltpu.VMEM((2, rows, NZ), F32),
            pltpu.VMEM((2, 2, 8, NZ), F32),
            pltpu.VMEM((4, 2, 8, NZ), F32),
            pltpu.VMEM((rows, NZ), F32),
            pltpu.VMEM((2, G, 8, NZ), F32),
            pltpu.VMEM((4, G, 8, NZ), F32),
            pltpu.VMEM((4, G, 8, NZ), F32),
            pltpu.VMEM((4, 8, NZ), F32),
            pltpu.VMEM((2, G, 8, NZ), F32),
            pltpu.VMEM((4, G, 8, NZ), F32),
            row_slots(4),
            row_slots(nzt * nk - 1),
            row_slots(nx * ny - 1),
            row_slots(nk - 1),
            row_slots(nx * ny * nzt - 1),
            pltpu.SMEM((slabs,), I32),
            pltpu.SMEM((3, Q, slabs), I32),
            pltpu.SMEM(energy.shape, F32),
            pltpu.SMEM((Q,), F32),
            pltpu.SMEM((Q,), I32),
            pltpu.SemaphoreType.DMA((8,)),
            pltpu.SemaphoreType.DMA((12,)),
            pltpu.SemaphoreType.DMA((12,)),
        ],
        compiler_params=pltpu.CompilerParams(collective_id=0, has_side_effects=True),
    )(
        coarse_rows,
        jnp.transpose(grain_ids, (1, 2, 0)),
        energy,
        order_params.reshape(Q, rows, NZ),
        layer_mask.reshape(rows, NZ),
        coarse_temp,
    )
    out = pl.pallas_call(
        write_out,
        out_shape=jax.ShapeDtypeStruct((Q, rows, NZ), F32),
        in_specs=[smem, vmem],
        out_specs=any_space,
        scratch_shapes=[pltpu.SemaphoreType.DMA((Q,))],
    )(pos, pltpu.with_memory_space_constraint(result, pltpu.VMEM))
    return out.reshape(Q, CX, CY, NZ)


def solution(mesh, torus=(4, 8, 4, 2)):
    placed = (
        P(None, "slab", "col", None),
        P("slab", "col", None),
        P("slab", "col", None),
        P(),
        P(),
        P(),
    )
    return jax.shard_map(
        functools.partial(per_device, torus),
        mesh=mesh,
        in_specs=placed,
        out_specs=P(None, "slab", "col", None),
        check_vma=False,
    )
```

```python
import functools

import jax
import jax.numpy as jnp
from jax import lax
from jax.experimental import pallas as pl
from jax.experimental.pallas import tpu as pltpu
from jax.sharding import PartitionSpec as P

Q = 16
G = 4
CX = 8
CY = 8
NZ = 256
CAP = 6
CYC = 4
NZC = 128
TIME_STEP = 0.05
EXACT = lax.Precision.HIGHEST
MESH = pl.DeviceIdType.MESH
F32 = jnp.float32
I32 = jnp.int32


def near(face):
    return 1 if face in (0, 2) else 0


def wait_for(ref, sem):
    pltpu.make_async_copy(ref, ref, sem).wait()


def kernel(
    torus,
    rows_hbm,
    ids_hbm,
    energy_hbm,
    fields_hbm,
    mask_hbm,
    coarse_hbm,
    out_ref,
    raw,
    mask,
    cb,
    cl,
    cr,
    pb,
    u_ref,
    v_ref,
    bf,
    nbi,
    nbg,
    rm,
    ym,
    yf,
    rf,
    ya,
    ra,
    st,
    ys,
    rs,
    sq,
    hy,
    ah,
    nh,
    nbh,
    y2,
    r2,
    ar_src,
    ar_1a,
    ar_1b,
    ar_2a,
    ar_2b,
    rows_s,
    ids_v,
    ids_s,
    energy_s,
    e_s,
    perm_s,
    pos_s,
    token,
    local_sem,
    send_sem,
    recv_sem,
):
    nx, nzt, ny, nk = torus
    slabs, cols = nx * nzt, ny * nk
    s = lax.axis_index("slab")
    c = lax.axis_index("col")
    tx, tz = s // nzt, s % nzt
    ty, tk = c // nk, c % nk
    planes_all = slabs * (CX // 2)
    col_low, col_high = jnp.maximum(c - 1, 0), jnp.minimum(c + 1, cols - 1)

    local = [
        pltpu.make_async_copy(ids_hbm.at[c], ids_v.at[0], local_sem.at[0]),
        pltpu.make_async_copy(ids_hbm.at[col_low], ids_v.at[1], local_sem.at[1]),
        pltpu.make_async_copy(ids_hbm.at[col_high], ids_v.at[2], local_sem.at[2]),
        pltpu.make_async_copy(energy_hbm, energy_s, local_sem.at[3]),
        pltpu.make_async_copy(rows_hbm, rows_s, local_sem.at[4]),
        pltpu.make_async_copy(fields_hbm, raw, local_sem.at[5]),
        pltpu.make_async_copy(mask_hbm, mask, local_sem.at[6]),
        pltpu.make_async_copy(coarse_hbm, cb.at[pl.ds(CAP, CAP)], local_sem.at[7]),
    ]
    for copy in local:
        copy.start()

    def halo_peer(ds, dc):
        return ((s + ds + slabs) % slabs, (c + dc + cols) % cols)

    def torus_peer(dx, dy, dz, dk):
        qx = (tx + dx) % nx if dx else tx
        qy = (ty + dy) % ny if dy else ty
        qz = (tz + dz) % nzt if dz else tz
        qk = (tk + dk) % nk if dk else tk
        return (qx * nzt + qz, qy * nk + qk)

    def far(offset):
        return -sum(min(d, n - d) for d, n in zip(offset, (nx, ny, nzt, nk)))

    def offsets(sx, sy, sz, sk):
        every = [
            (a, b, d, e)
            for a in range(sx)
            for b in range(sy)
            for d in range(sz)
            for e in range(sk)
            if (a, b, d, e) != (0, 0, 0, 0)
        ]
        return sorted(every, key=far)

    halo_offsets = [(a, b) for a in (-1, 0, 1) for b in (-1, 0, 1) if (a, b) != (0, 0)]
    group_xy = offsets(nx, ny, 1, 1)
    group_k = offsets(1, 1, 1, nk)
    group_xyz = offsets(nx, ny, nzt, 1)

    def signal(sem, peer):
        pl.semaphore_signal(sem, inc=1, device_id=peer, device_id_type=MESH)

    steps = [(1, 0, 0), (nx - 1, 0, 0), (0, 1, 0), (0, ny - 1, 0), (0, 0, 1), (0, 0, nzt - 1)]
    peers = [halo_peer(*o) for o in halo_offsets]
    peers += [torus_peer(*o, 0) for o in steps]
    peers += [torus_peer(*o, 1) for o in steps[4:]]
    barrier = pltpu.get_barrier_semaphore()
    for peer in peers:
        signal(barrier, peer)

    face_offset = ((-1, 0), (1, 0), (0, -1), (0, 1))
    has_flag = (s > 0, s < slabs - 1, c > 0, c < cols - 1)
    has = [jnp.where(flag, 1.0, 0.0).astype(F32) for flag in has_flag]

    def send(src, dst, peer, sem):
        pltpu.make_async_remote_copy(
            src_ref=src,
            dst_ref=dst,
            send_sem=send_sem.at[sem],
            recv_sem=recv_sem.at[sem],
            device_id=peer,
            device_id_type=MESH,
        ).start()

    sub = lax.broadcasted_iota(I32, (CY, NZ), 0)
    lane = lax.broadcasted_iota(I32, (CY, NZ), 1)
    zero_slab = jnp.zeros((CY, NZ), F32)

    def column(view, start):
        rows = jnp.broadcast_to(view[pl.ds(start, 1), :], (CX, NZ))
        for x in range(1, CX):
            rows = jnp.where(sub == x, view[pl.ds(start + CY * x, 1), :], rows)
        return rows

    sub_i = lax.broadcasted_iota(I32, (Q, 4 * Q), 0)
    lane_i = lax.broadcasted_iota(I32, (Q, 4 * Q), 1)
    lane_s = lax.broadcasted_iota(I32, (Q, slabs), 1)
    sub_q = lax.broadcasted_iota(I32, (Q, Q), 0)
    lane_q = lax.broadcasted_iota(I32, (Q, Q), 1)

    def ids_of(which, at):
        picked = jnp.where(lane_s == at, ids_v[which], 0)
        return jnp.sum(picked, axis=1, keepdims=True)

    def as_row(values):
        return jnp.sum(jnp.where(sub_q == lane_q, values, 0), axis=0, keepdims=True)

    for copy in local[:3]:
        copy.wait()
    own = ids_of(0, s)
    beside = (
        jnp.where(has_flag[0], ids_of(0, jnp.maximum(s - 1, 0)), -1),
        jnp.where(has_flag[1], ids_of(0, jnp.minimum(s + 1, slabs - 1)), -1),
        jnp.where(has_flag[2], ids_of(1, s), -1),
        jnp.where(has_flag[3], ids_of(2, s), -1),
    )
    face_i = lane_i >> 4
    every = jnp.where(
        face_i < 2,
        jnp.where(face_i == 0, beside[0], beside[1]),
        jnp.where(face_i == 2, beside[2], beside[3]),
    )
    every = jnp.sum(jnp.where((lane_i & 15) == sub_i, every, 0), axis=0, keepdims=True)
    found = jnp.sum(jnp.where(own == every, face_i + 1, 0), axis=1, keepdims=True)
    free = jnp.where(found == 0, own, 65535)
    free_rank = jnp.sum(jnp.where(as_row(free) < own, 1, 0), axis=1, keepdims=True)
    first_free = jnp.where(s == 0, 0, jnp.where(s == slabs - 1, 1, jnp.where(c == 0, 2, 3)))
    last_free = jnp.where(c == 0, 2, 3)
    place = jnp.where(free_rank < G, first_free, last_free)
    key = jnp.where(found == 0, place, found - 1) * 65536 + own
    position = jnp.sum(jnp.where(as_row(key) < key, 1, 0), axis=1, keepdims=True)
    order = jnp.sum(jnp.where(position == lane_q, sub_q, 0), axis=0, keepdims=True)
    order = jnp.minimum(order, Q - 1)
    own_row = as_row(own)
    position_row = as_row(position)
    for p in range(Q):
        perm_s[p] = order[0, p]

    local[5].wait()
    for p in range(Q):
        u_ref[p, 8:72, :] = raw[perm_s[p]]
    for j in range(G):
        yf[0, j] = column(u_ref.at[2 * G + j], 8)
        yf[1, j] = column(u_ref.at[3 * G + j], 15)
    local[6].wait()
    for k in range(2):
        ym[0, 8 * k : 8 * k + 8, :] = column(mask, k)
        ym[1, 8 * k : 8 * k + 8, :] = column(mask, 6 + k)

    pl.semaphore_wait(barrier, len(peers))
    for o in steps:
        signal(token.at[0], torus_peer(*o, 0))

    for ds, dc in halo_offsets:
        at = pl.ds((1 - ds) * CAP, CAP)
        if dc == 0:
            send(coarse_hbm, cb.at[at], halo_peer(ds, dc), 0)
        else:
            send(coarse_hbm, (cl if dc > 0 else cr).at[at], halo_peer(ds, dc), 1 if dc > 0 else 2)
    field_src = (
        u_ref.at[pl.ds(0, G), pl.ds(8, 8)],
        u_ref.at[pl.ds(G, G), pl.ds(64, 8)],
        yf.at[0],
        yf.at[1],
    )
    mask_src = (mask.at[pl.ds(0, 16)], mask.at[pl.ds(48, 16)], ym.at[0], ym.at[1])
    for face in range(4):
        send(field_src[face], rf.at[face ^ 1], halo_peer(*face_offset[face]), 3)
    for face in range(4):
        send(mask_src[face], rm.at[face ^ 1], halo_peer(*face_offset[face]), 4)

    for q in range(Q):
        for ref in (u_ref, v_ref):
            ref[q, 0:8, :] = zero_slab
            ref[q, 72:80, :] = zero_slab
    pl.semaphore_wait(token.at[0], len(steps))
    twos = [(2, 0, 0), (0, 2, 0), (0, 0, 2), (0, 0, nzt - 2)]
    for o in twos:
        signal(token.at[1], torus_peer(*o, 0))
    local[3].wait()
    for q in range(Q):
        pos_s[q] = position_row[0, q]
        ids_s[q] = own_row[0, q]
    for p in range(Q):
        e_s[p] = energy_s[ids_s[perm_s[p]]]
    e_total = e_s[0]
    for p in range(1, Q):
        e_total += e_s[p]
    local[4].wait()
    start_own = jnp.int32(0)
    for i in range(slabs):
        start_own += jnp.where(i < s, rows_s[i], 0)
    end_own = start_own + rows_s[s]
    start_prev = start_own - rows_s[jnp.maximum(s - 1, 0)]

    def sides(f, low_row, high_row):
        total = jnp.where(sub == 0, low_row, pltpu.roll(f, 1, 0))
        total += jnp.where(sub == CY - 1, high_row, pltpu.roll(f, CY - 1, 0))
        total += jnp.where(lane == 0, 0.0, pltpu.roll(f, 1, 1))
        total += jnp.where(lane == NZ - 1, 0.0, pltpu.roll(f, NZ - 1, 1))
        return total

    def inside(src, squares):
        def body(x, carry):
            r = pl.multiple_of(8 * x, 8)
            total = zero_slab
            for q in range(Q):
                f = src[q, pl.ds(r + 8, 8), :]
                around = src[q, pl.ds(r, 8), :] + src[q, pl.ds(r + 16, 8), :]
                raw[q, pl.ds(r, 8), :] = around + sides(f, 0.0, 0.0)
                if squares:
                    total += f * f
            if squares:
                sq[pl.ds(r, 8), :] = total
            return carry

        lax.fori_loop(0, CX, body, 0)

    def add_faces(halo):
        for j in range(G):
            raw[j, 0:8, :] = raw[j, 0:8, :] + halo(0, j)
            raw[G + j, 56:64, :] = raw[G + j, 56:64, :] + halo(1, j)
            low, high = halo(2, j), halo(3, j)
            for x in range(CX):
                at = slice(8 * x, 8 * x + 8)
                row = jnp.where(sub == 0, low[x : x + 1, :], 0.0)
                raw[2 * G + j, at, :] = raw[2 * G + j, at, :] + row
                row = jnp.where(sub == CY - 1, high[x : x + 1, :], 0.0)
                raw[3 * G + j, at, :] = raw[3 * G + j, at, :] + row

    inside(u_ref, True)
    pl.semaphore_wait(token.at[1], len(twos))
    for o in group_xy:
        signal(token.at[2], torus_peer(*o))

    out_row = lax.broadcasted_iota(I32, (128, 64), 0)
    in_row = lax.broadcasted_iota(I32, (128, 64), 1)
    high = out_row >> 3
    low = out_row & 7
    along = jnp.where(
        out_row < 64,
        high,
        jnp.where(out_row < 80, high - 10, jnp.where(out_row < 96, high - 2, low)),
    )
    across = jnp.where(out_row < 96, low, jnp.where(out_row < 112, high - 14, high - 6))

    def node_weight(fine, node):
        twice = 2 * fine - 1
        lower = twice >> 2
        w = (twice - 4 * lower).astype(F32) * 0.25
        return jnp.where(node == lower + 2, 1.0 - w, jnp.where(node == lower + 3, w, 0.0))

    weight_xy = node_weight(along, in_row >> 3) * node_weight(across, in_row & 7)
    node_z = lax.broadcasted_iota(I32, (NZC, NZ), 0)
    fine_z = lax.broadcasted_iota(I32, (NZC, NZ), 1)
    lower_z = (2 * fine_z - 1) >> 2
    w_z = (2 * fine_z - 1 - 4 * lower_z).astype(F32) * 0.25
    weight_z = jnp.where(node_z == jnp.clip(lower_z, 0, NZC - 1), 1.0 - w_z, 0.0) + jnp.where(
        node_z == jnp.clip(lower_z + 1, 0, NZC - 1), w_z, 0.0
    )

    local[7].wait()
    wait_for(cb.at[pl.ds(0, 2 * CAP)], recv_sem.at[0])
    wait_for(cl, recv_sem.at[1])
    wait_for(cr, recv_sem.at[2])
    for i in range(8):
        plane = jnp.clip(s * (CX // 2) - 2 + i, 0, planes_all - 1)
        flat = jnp.where(
            plane < start_own,
            plane - start_prev,
            jnp.where(plane < end_own, CAP + plane - start_own, 2 * CAP + plane - end_own),
        )
        flat = jnp.clip(flat, 0, 3 * CAP - 1)
        mine = cb[flat]
        left = cl[flat, CYC - 2 : CYC, :]
        right = cr[flat, 0:2, :]
        pb[8 * i : 8 * i + 2, :] = jnp.where(c == 0, mine[0:1], left)
        pb[8 * i + 2 : 8 * i + 6, :] = mine
        pb[8 * i + 6 : 8 * i + 8, :] = jnp.where(c == cols - 1, mine[CYC - 1 : CYC], right)
    profile = jnp.dot(weight_xy, pb[...], precision=EXACT, preferred_element_type=F32)
    profile = jnp.dot(profile, weight_z, precision=EXACT, preferred_element_type=F32)
    scaled = TIME_STEP * jnp.exp(2.0 * (profile - 1.0))
    bf[0:64, :] = scaled[0:64] * mask[...].astype(F32)
    bf[64:128, :] = scaled[64:128]

    wait_for(rf, recv_sem.at[3])
    add_faces(lambda face, j: rf[face, j] * has[face])

    def near_b(face):
        at = 64 + 16 * face + 8 * near(face)
        return bf[at : at + 8, :]

    def react(src, dst, offset, shift, sums):
        def body(x, carry):
            r = pl.multiple_of(8 * x, 8)
            b = bf[pl.ds(r, 8), :]
            if shift is None:
                squares = sq[pl.ds(r, 8), :]
            else:
                m, extra = shift
                mb = m * b
                squares = st[0, pl.ds(r, 8), :] + mb * (16.0 * mb - 2.0 * st[1, pl.ds(r, 8), :])
                base = [extra + m * nbg[g, pl.ds(r, 8), :] for g in range(4)]
            common = 5.0 + 3.0 * squares
            acc = [zero_slab] * 6
            for q in range(Q):
                p = pos_s[q] if dst is out_ref else q
                e = e_s[p]
                f = src[p, pl.ds(r + 8, 8), :]
                if shift is not None:
                    f = f - mb
                force = f * ((common - e) + f * (e - 2.0 * f))
                if sums and shift is None and src is not v_ref and offset is not None:
                    around = raw[q, pl.ds(r, 8), :]
                elif shift is None:
                    low_row = hy[0, q - 2 * G, pl.ds(x, 1), :] if q // G == 2 else 0.0
                    high_row = hy[1, q - 3 * G, pl.ds(x, 1), :] if q // G == 3 else 0.0
                    around = src[q, pl.ds(r, 8), :] + src[q, pl.ds(r + 16, 8), :]
                    around += sides(f, low_row, high_row)
                elif dst is out_ref:
                    around = raw[p, pl.ds(r, 8), :] - (extra + m * nbg[p >> 2, pl.ds(r, 8), :])
                else:
                    around = raw[q, pl.ds(r, 8), :] - base[q // G]
                force = force - around
                a = f - b * force
                if sums:
                    square = a * a
                    ea = e * a
                    step = (force, a, square, square * a, ea, ea * a)
                    acc = [total + value for total, value in zip(acc, step)]
                elif dst is u_ref:
                    acc[0] += a * a
                dst[q, pl.ds(r + (offset or 8 if dst is not out_ref else 0), 8), :] = a
            if not sums:
                if dst is u_ref:
                    sq[pl.ds(r, 8), :] = acc[0]
                return carry
            force_all, t1, t2, t3, te, te2 = acc
            st[0, pl.ds(r, 8), :] = t2
            st[1, pl.ds(r, 8), :] = t1
            total, k0, k1, k2 = carry
            b2 = b * b
            total += b * force_all
            k0 += b * (t1 * (5.0 + 3.0 * t2) - te + te2 - 2.0 * t3) - t1 * nbi[pl.ds(r, 8), :]
            k1 += b2 * (e_total - 80.0 - 42.0 * t2 - 6.0 * t1 * t1 - 2.0 * te)
            k2 += b2 * b * (138.0 * t1 + e_total)
            return total, k0, k1, k2

        start = (zero_slab,) * 4 if sums else 0
        return lax.fori_loop(0, CX, body, start)

    sum_b = zero_slab
    sum_b4 = zero_slab
    sum_bnb = zero_slab
    for x in range(CX):
        b = bf[8 * x : 8 * x + 8, :]
        around = sides(b, 0.0, 0.0)
        if x > 0:
            around += bf[8 * x - 8 : 8 * x, :]
        if x < CX - 1:
            around += bf[8 * x + 8 : 8 * x + 16, :]
        nbi[8 * x : 8 * x + 8, :] = around
        square = b * b
        sum_b += b
        sum_b4 += square * square
        sum_bnb += 16.0 * b * around

    parts = react(u_ref, v_ref, 8, None, True)

    wait_for(rm, recv_sem.at[4])
    for face in range(4):
        at = 64 + 16 * face
        bf[at : at + 16, :] = bf[at : at + 16, :] * rm[face].astype(F32) * has[face]
    face_b = (bf[0:8, :], bf[56:64, :], column(bf, 0), column(bf, 7))
    for face in range(4):
        sum_bnb += 4.0 * face_b[face] * near_b(face)

    for j in range(G):
        for k in range(2):
            ya[0, j, 8 * k : 8 * k + 8, :] = column(v_ref.at[2 * G + j], 8 + k)
            ya[1, j, 8 * k : 8 * k + 8, :] = column(v_ref.at[3 * G + j], 14 + k)

    lane_1 = lax.broadcasted_iota(I32, (1, 128), 1)

    def put_row(at, parts, faces):
        total, k0, k1, k2 = parts
        for face in range(4):
            layer = faces[face][0]
            for j in range(1, G):
                layer = layer + faces[face][j]
            k0 -= layer * near_b(face)
        every = (sum_b, total, k0, k1 + sum_bnb, k2, -736.0 * sum_b4)
        tile = jnp.zeros((8, 128), F32)
        for k, part in enumerate(every):
            half = part[:, :128] + part[:, 128:]
            tile = jnp.where(sub[:, :128] == k, jnp.sum(half, axis=0, keepdims=True), tile)
        tile = jnp.where(sub[:, :128] == lane[:, :128], jnp.sum(tile, axis=1, keepdims=True), 0.0)
        row = jnp.sum(tile, axis=0, keepdims=True)
        ar_src[at] = row

    def spread(at, group, landing, sem):
        for k, offset in enumerate(group):
            send(ar_src.at[at], landing.at[k], torus_peer(*offset), sem)

    def gathered(at, landing, sem):
        wait_for(landing, recv_sem.at[sem])
        return ar_src[at] + jnp.sum(landing[...], axis=0)

    def two_multipliers(row):
        got = [
            jnp.sum(jnp.where(lane_1 == k, row, 0.0), axis=1, keepdims=True) for k in range(6)
        ]
        inverse = -1.0 / (16.0 * got[0])
        m_a = got[1] * inverse
        m_b = (got[2] + m_a * (got[3] + m_a * (got[4] + m_a * got[5]))) * inverse
        return jnp.broadcast_to(m_a, (CY, NZ)), jnp.broadcast_to(m_b, (CY, NZ))

    put_row(
        0,
        parts,
        (
            [v_ref[j, 8:16, :] for j in range(G)],
            [v_ref[G + j, 64:72, :] for j in range(G)],
            [ya[0, j, 0:8, :] for j in range(G)],
            [ya[1, j, 8:16, :] for j in range(G)],
        ),
    )
    spread(0, group_k, ar_1a, 5)

    for k in range(2):
        ys[0, k] = column(st.at[k], 0)
        ys[1, k] = column(st.at[k], 7)
    pl.semaphore_wait(token.at[2], len(group_xy))
    ar_src[1] = gathered(0, ar_1a, 5)
    spread(1, group_xyz, ar_1b, 8)
    deep = (
        v_ref.at[pl.ds(0, G), pl.ds(8, 16)],
        v_ref.at[pl.ds(G, G), pl.ds(56, 16)],
        ya.at[0],
        ya.at[1],
    )
    flat = (st.at[:, pl.ds(0, 8)], st.at[:, pl.ds(56, 8)], ys.at[0], ys.at[1])
    for face in range(4):
        peer = halo_peer(*face_offset[face])
        send(deep[face], ra.at[face ^ 1], peer, 6)
        send(flat[face], rs.at[face ^ 1], peer, 7)
    inside(v_ref, False)
    for x in range(CX):
        at = slice(8 * x, 8 * x + 8)
        here = nbi[at, :]
        nbg[0, at, :] = here + near_b(0) if x == 0 else here
        nbg[1, at, :] = here + near_b(1) if x == CX - 1 else here
        nbg[2, at, :] = here + jnp.where(sub == 0, near_b(2)[x : x + 1, :], 0.0)
        nbg[3, at, :] = here + jnp.where(sub == CY - 1, near_b(3)[x : x + 1, :], 0.0)

    wait_for(ra, recv_sem.at[6])
    wait_for(rs, recv_sem.at[7])
    for face in range(4):
        here, beyond = 8 * near(face), 8 * (1 - near(face))
        at = 64 + 16 * face
        b = near_b(face)
        nbh[face] = bf[at + beyond : at + beyond + 8, :] + face_b[face] + sides(b, 0.0, 0.0)
        for j in range(G):
            value = ra[face, j, here : here + 8, :] * has[face]
            ah[face, j] = value
            if face == 0:
                inner = v_ref[j, 8:16, :]
            elif face == 1:
                inner = v_ref[G + j, 64:72, :]
            elif face == 2:
                inner = ya[0, j, 0:8, :]
            else:
                inner = ya[1, j, 8:16, :]
            outer = ra[face, j, beyond : beyond + 8, :]
            nh[face, j] = outer + inner + sides(value, 0.0, 0.0)
    add_faces(lambda face, j: ah[face, j])

    m0, m1 = two_multipliers(gathered(1, ar_1b, 8))

    wait_for(rf, send_sem.at[3])
    for face in range(4):
        b = near_b(face)
        mb = m0 * b
        squares = rs[face, 0] + mb * (16.0 * mb - 2.0 * rs[face, 1])
        common = 5.0 + 3.0 * squares
        base = m1 + m0 * nbh[face]
        for j in range(G):
            e = e_s[face * G + j]
            f = ah[face, j] - mb
            force = f * ((common - e) + f * (e - 2.0 * f)) - (nh[face, j] - base)
            value = f - b * force
            if face == 0:
                u_ref[j, 0:8, :] = value
            elif face == 1:
                u_ref[G + j, 72:80, :] = value
            else:
                hy[face - 2, j] = value
    react(v_ref, u_ref, 8, (m0, m1), False)

    wait_for(ra, send_sem.at[6])
    wait_for(rs, send_sem.at[7])
    parts = react(u_ref, v_ref, None, None, True)
    for j in range(G):
        y2[0, j] = column(v_ref.at[2 * G + j], 8)
        y2[1, j] = column(v_ref.at[3 * G + j], 15)
    put_row(
        2,
        parts,
        (
            [v_ref[j, 8:16, :] for j in range(G)],
            [v_ref[G + j, 64:72, :] for j in range(G)],
            [y2[0, j] for j in range(G)],
            [y2[1, j] for j in range(G)],
        ),
    )
    spread(2, group_k, ar_2a, 9)
    ar_src[3] = gathered(2, ar_2a, 9)
    spread(3, group_xyz, ar_2b, 10)
    shallow = (
        v_ref.at[pl.ds(0, G), pl.ds(8, 8)],
        v_ref.at[pl.ds(G, G), pl.ds(64, 8)],
        y2.at[0],
        y2.at[1],
    )
    for face in range(4):
        send(shallow[face], r2.at[face ^ 1], halo_peer(*face_offset[face]), 11)
    inside(v_ref, False)
    wait_for(r2, recv_sem.at[11])
    add_faces(lambda face, j: r2[face, j] * has[face])
    wait_for(cb.at[pl.ds(0, 2 * CAP)], send_sem.at[0])
    wait_for(cl, send_sem.at[1])
    wait_for(cr, send_sem.at[2])
    wait_for(rm, send_sem.at[4])
    wait_for(ar_1a, send_sem.at[5])
    wait_for(ar_1b, send_sem.at[8])
    wait_for(ar_2a, send_sem.at[9])
    wait_for(r2, send_sem.at[11])

    m2, m3 = two_multipliers(gathered(3, ar_2b, 10))
    react(v_ref, out_ref, 0, (m2, m3), False)
    wait_for(ar_2b, send_sem.at[10])


def write_out(result, out_hbm, sem):
    copy = pltpu.make_async_copy(result, out_hbm, sem.at[0])
    copy.start()
    copy.wait()


def per_device(torus, order_params, layer_mask, coarse_temp, coarse_rows, grain_ids, energy):
    any_space = pl.BlockSpec(memory_space=pl.ANY)
    vmem = pl.BlockSpec(memory_space=pltpu.VMEM)
    nx, nzt, ny, nk = torus
    slabs = nx * nzt
    rows = CX * CY

    def row_slots(count):
        return pltpu.VMEM((count, 1, 128), F32)

    result = pl.pallas_call(
        functools.partial(kernel, torus),
        out_shape=pltpu.VMEM((Q, rows, NZ), F32),
        in_specs=[any_space] * 6,
        out_specs=vmem,
        scratch_shapes=[
            pltpu.VMEM((Q, rows, NZ), F32),
            pltpu.VMEM((rows, NZ), I32),
            pltpu.VMEM((3 * CAP, CYC, NZC), F32),
            pltpu.VMEM((3 * CAP, CYC, NZC), F32),
            pltpu.VMEM((3 * CAP, CYC, NZC), F32),
            pltpu.VMEM((64, NZC), F32),
            pltpu.VMEM((Q, rows + 16, NZ), F32),
            pltpu.VMEM((Q, rows + 16, NZ), F32),
            pltpu.VMEM((128, NZ), F32),
            pltpu.VMEM((rows, NZ), F32),
            pltpu.VMEM((4, rows, NZ), F32),
            pltpu.VMEM((4, 16, NZ), I32),
            pltpu.VMEM((2, 16, NZ), I32),
            pltpu.VMEM((2, G, 8, NZ), F32),
            pltpu.VMEM((4, G, 8, NZ), F32),
            pltpu.VMEM((2, G, 16, NZ), F32),
            pltpu.VMEM((4, G, 16, NZ), F32),
            pltpu.VMEM((2, rows, NZ), F32),
            pltpu.VMEM((2, 2, 8, NZ), F32),
            pltpu.VMEM((4, 2, 8, NZ), F32),
            pltpu.VMEM((rows, NZ), F32),
            pltpu.VMEM((2, G, 8, NZ), F32),
            pltpu.VMEM((4, G, 8, NZ), F32),
            pltpu.VMEM((4, G, 8, NZ), F32),
            pltpu.VMEM((4, 8, NZ), F32),
            pltpu.VMEM((2, G, 8, NZ), F32),
            pltpu.VMEM((4, G, 8, NZ), F32),
            row_slots(4),
            row_slots(nk - 1),
            row_slots(nx * ny * nzt - 1),
            row_slots(nk - 1),
            row_slots(nx * ny * nzt - 1),
            pltpu.SMEM((slabs,), I32),
            pltpu.VMEM((3, Q, slabs), I32),
            pltpu.SMEM((Q,), I32),
            pltpu.SMEM(energy.shape, F32),
            pltpu.SMEM((Q,), F32),
            pltpu.SMEM((Q,), I32),
            pltpu.SMEM((Q,), I32),
            pltpu.SemaphoreType.REGULAR((3,)),
            pltpu.SemaphoreType.DMA((8,)),
            pltpu.SemaphoreType.DMA((12,)),
            pltpu.SemaphoreType.DMA((12,)),
        ],
        compiler_params=pltpu.CompilerParams(collective_id=0, has_side_effects=True),
    )(
        coarse_rows,
        jnp.transpose(grain_ids, (1, 2, 0)),
        energy,
        order_params.reshape(Q, rows, NZ),
        layer_mask.reshape(rows, NZ),
        coarse_temp,
    )
    out = pl.pallas_call(
        write_out,
        out_shape=jax.ShapeDtypeStruct((Q, rows, NZ), F32),
        in_specs=[vmem],
        out_specs=any_space,
        scratch_shapes=[pltpu.SemaphoreType.DMA((1,))],
    )(pltpu.with_memory_space_constraint(result, pltpu.VMEM))
    return out.reshape(Q, CX, CY, NZ)


def solution(mesh, torus=(4, 8, 4, 2)):
    placed = (
        P(None, "slab", "col", None),
        P("slab", "col", None),
        P("slab", "col", None),
        P(),
        P(),
        P(),
    )
    return jax.shard_map(
        functools.partial(per_device, torus),
        mesh=mesh,
        in_specs=placed,
        out_specs=P(None, "slab", "col", None),
        check_vma=False,
    )
```

```python
import functools

import jax
import jax.numpy as jnp
from jax import lax
from jax.experimental import pallas as pl
from jax.experimental.pallas import tpu as pltpu
from jax.sharding import PartitionSpec as P

Q = 16
G = 4
CX = 8
CY = 8
NZ = 256
CAP = 6
CYC = 4
NZC = 128
TIME_STEP = 0.05
MESH = pl.DeviceIdType.MESH
F32 = jnp.float32
I32 = jnp.int32
BF16 = jnp.bfloat16


def near(face):
    return 1 if face in (0, 2) else 0


def wait_for(ref, sem):
    pltpu.make_async_copy(ref, ref, sem).wait()


def kernel(
    torus,
    rows_hbm,
    ids_hbm,
    energy_hbm,
    fields_hbm,
    mask_hbm,
    coarse_hbm,
    last_a,
    last_n,
    last_b,
    last_e,
    last_s,
    last_w,
    last_m,
    raw,
    mask,
    cb,
    cl,
    cr,
    pb,
    u_ref,
    v_ref,
    bf,
    nbi,
    nbg,
    rm,
    ym,
    yf,
    rf,
    ya,
    ra,
    st,
    ys,
    rs,
    sq,
    hy,
    ah,
    nh,
    nbh,
    y2,
    r2,
    ar_src,
    ar_1a,
    ar_2a,
    ar_2b,
    rows_s,
    ids_v,
    ids_s,
    energy_s,
    e_s,
    perm_s,
    pos_s,
    token,
    local_sem,
    send_sem,
    recv_sem,
):
    nx, nzt, ny, nk = torus
    slabs, cols = nx * nzt, ny * nk
    local = [
        pltpu.make_async_copy(energy_hbm, energy_s, local_sem.at[3]),
        pltpu.make_async_copy(rows_hbm, rows_s, local_sem.at[4]),
        pltpu.make_async_copy(fields_hbm, raw, local_sem.at[5]),
        pltpu.make_async_copy(mask_hbm, mask, local_sem.at[6]),
        pltpu.make_async_copy(coarse_hbm, cb.at[pl.ds(CAP, CAP)], local_sem.at[7]),
    ]
    for copy in local:
        copy.start()
    s = lax.axis_index("slab")
    c = lax.axis_index("col")
    tx, tz = s // nzt, s % nzt
    ty, tk = c // nk, c % nk
    planes_all = slabs * (CX // 2)
    col_low, col_high = jnp.maximum(c - 1, 0), jnp.minimum(c + 1, cols - 1)

    local_ids = [
        pltpu.make_async_copy(ids_hbm.at[c], ids_v.at[0], local_sem.at[0]),
        pltpu.make_async_copy(ids_hbm.at[col_low], ids_v.at[1], local_sem.at[1]),
        pltpu.make_async_copy(ids_hbm.at[col_high], ids_v.at[2], local_sem.at[2]),
    ]
    for copy in local_ids:
        copy.start()
    local = local_ids + local

    def halo_peer(ds, dc):
        return ((s + ds + slabs) % slabs, (c + dc + cols) % cols)

    def torus_peer(dx, dy, dz, dk):
        qx = (tx + dx) % nx if dx else tx
        qy = (ty + dy) % ny if dy else ty
        qz = (tz + dz) % nzt if dz else tz
        qk = (tk + dk) % nk if dk else tk
        return (qx * nzt + qz, qy * nk + qk)

    def far(offset):
        return -sum(min(d, n - d) for d, n in zip(offset, (nx, ny, nzt, nk)))

    def offsets(sx, sy, sz, sk):
        every = [
            (a, b, d, e)
            for a in range(sx)
            for b in range(sy)
            for d in range(sz)
            for e in range(sk)
            if (a, b, d, e) != (0, 0, 0, 0)
        ]
        return sorted(every, key=far)

    halo_offsets = [(a, b) for a in (-1, 0, 1) for b in (-1, 0, 1) if (a, b) != (0, 0)]
    group_xy = offsets(nx, ny, 1, 1)
    group_k = offsets(1, 1, 1, nk)
    group_all = offsets(nx, ny, nzt, nk)
    group_xyz = offsets(nx, ny, nzt, 1)

    def signal(sem, peer):
        pl.semaphore_signal(sem, inc=1, device_id=peer, device_id_type=MESH)

    steps = [(1, 0, 0), (nx - 1, 0, 0), (0, 1, 0), (0, ny - 1, 0), (0, 0, 1), (0, 0, nzt - 1)]
    peers = [halo_peer(*o) for o in halo_offsets]
    peers += [torus_peer(*o, 0) for o in steps]
    peers += [torus_peer(*o, 1) for o in steps[4:]]
    barrier = pltpu.get_barrier_semaphore()
    for peer in peers:
        signal(barrier, peer)

    face_offset = ((-1, 0), (1, 0), (0, -1), (0, 1))
    has_flag = (s > 0, s < slabs - 1, c > 0, c < cols - 1)
    has = [jnp.where(flag, 1.0, 0.0).astype(F32) for flag in has_flag]

    def send(src, dst, peer, sem):
        pltpu.make_async_remote_copy(
            src_ref=src,
            dst_ref=dst,
            send_sem=send_sem.at[sem],
            recv_sem=recv_sem.at[sem],
            device_id=peer,
            device_id_type=MESH,
        ).start()

    sub = lax.broadcasted_iota(I32, (CY, NZ), 0)
    lane = lax.broadcasted_iota(I32, (CY, NZ), 1)
    zero_slab = jnp.zeros((CY, NZ), F32)

    def column(view, start):
        rows = jnp.broadcast_to(view[pl.ds(start, 1), :], (CX, NZ))
        for x in range(1, CX):
            rows = jnp.where(sub == x, view[pl.ds(start + CY * x, 1), :], rows)
        return rows

    sub_i = lax.broadcasted_iota(I32, (Q, 4 * Q), 0)
    lane_i = lax.broadcasted_iota(I32, (Q, 4 * Q), 1)
    lane_s = lax.broadcasted_iota(I32, (Q, slabs), 1)
    sub_q = lax.broadcasted_iota(I32, (Q, Q), 0)
    lane_q = lax.broadcasted_iota(I32, (Q, Q), 1)

    def ids_of(which, at):
        picked = jnp.where(lane_s == at, ids_v[which], 0)
        return jnp.sum(picked, axis=1, keepdims=True)

    def as_row(values):
        return jnp.sum(jnp.where(sub_q == lane_q, values, 0), axis=0, keepdims=True)

    for copy in local[:3]:
        copy.wait()
    own = ids_of(0, s)
    beside = (
        jnp.where(has_flag[0], ids_of(0, jnp.maximum(s - 1, 0)), -1),
        jnp.where(has_flag[1], ids_of(0, jnp.minimum(s + 1, slabs - 1)), -1),
        jnp.where(has_flag[2], ids_of(1, s), -1),
        jnp.where(has_flag[3], ids_of(2, s), -1),
    )
    face_i = lane_i >> 4
    every = jnp.where(
        face_i < 2,
        jnp.where(face_i == 0, beside[0], beside[1]),
        jnp.where(face_i == 2, beside[2], beside[3]),
    )
    every = jnp.sum(jnp.where((lane_i & 15) == sub_i, every, 0), axis=0, keepdims=True)
    found = jnp.sum(jnp.where(own == every, face_i + 1, 0), axis=1, keepdims=True)
    free = jnp.where(found == 0, own, 65535)
    free_rank = jnp.sum(jnp.where(as_row(free) < own, 1, 0), axis=1, keepdims=True)
    first_free = jnp.where(s == 0, 0, jnp.where(s == slabs - 1, 1, jnp.where(c == 0, 2, 3)))
    last_free = jnp.where(c == 0, 2, 3)
    place = jnp.where(free_rank < G, first_free, last_free)
    key = jnp.where(found == 0, place, found - 1) * 65536 + own
    position = jnp.sum(jnp.where(as_row(key) < key, 1, 0), axis=1, keepdims=True)
    order = jnp.sum(jnp.where(position == lane_q, sub_q, 0), axis=0, keepdims=True)
    order = jnp.minimum(order, Q - 1)
    own_row = as_row(own)
    position_row = as_row(position)
    for p in range(Q):
        perm_s[p] = order[0, p]

    local[5].wait()
    for p in range(Q):
        u_ref[p, 8:72, :] = raw[perm_s[p]]
    for j in range(G):
        yf[0, j] = column(u_ref.at[2 * G + j], 8)
        yf[1, j] = column(u_ref.at[3 * G + j], 15)
    local[6].wait()
    for k in range(2):
        ym[0, 8 * k : 8 * k + 8, :] = column(mask, k)
        ym[1, 8 * k : 8 * k + 8, :] = column(mask, 6 + k)

    pl.semaphore_wait(barrier, len(peers))
    for o in steps:
        signal(token.at[0], torus_peer(*o, 0))

    for ds, dc in halo_offsets:
        at = pl.ds((1 - ds) * CAP, CAP)
        if dc == 0:
            send(coarse_hbm, cb.at[at], halo_peer(ds, dc), 0)
        else:
            send(coarse_hbm, (cl if dc > 0 else cr).at[at], halo_peer(ds, dc), 1 if dc > 0 else 2)
    field_src = (
        u_ref.at[pl.ds(0, G), pl.ds(8, 8)],
        u_ref.at[pl.ds(G, G), pl.ds(64, 8)],
        yf.at[0],
        yf.at[1],
    )
    mask_src = (mask.at[pl.ds(0, 16)], mask.at[pl.ds(48, 16)], ym.at[0], ym.at[1])
    for face in range(4):
        send(field_src[face], rf.at[face ^ 1], halo_peer(*face_offset[face]), 3)
    for face in range(4):
        send(mask_src[face], rm.at[face ^ 1], halo_peer(*face_offset[face]), 4)

    for q in range(Q):
        for ref in (u_ref, v_ref):
            ref[q, 0:8, :] = zero_slab
            ref[q, 72:80, :] = zero_slab
    pl.semaphore_wait(token.at[0], len(steps))
    twos = [(2, 0, 0), (0, 2, 0), (0, 0, 2), (0, 0, nzt - 2)]
    for o in twos:
        signal(token.at[1], torus_peer(*o, 0))
    local[3].wait()
    for q in range(Q):
        pos_s[q] = position_row[0, q]
        ids_s[q] = own_row[0, q]
    for p in range(Q):
        e_s[p] = energy_s[ids_s[perm_s[p]]]
    e_total = e_s[0]
    for p in range(1, Q):
        e_total += e_s[p]
    local[4].wait()
    start_own = jnp.int32(0)
    for i in range(slabs):
        start_own += jnp.where(i < s, rows_s[i], 0)
    end_own = start_own + rows_s[s]
    start_prev = start_own - rows_s[jnp.maximum(s - 1, 0)]

    def sides(f, low_row, high_row):
        total = jnp.where(sub == 0, low_row, pltpu.roll(f, 1, 0))
        total += jnp.where(sub == CY - 1, high_row, pltpu.roll(f, CY - 1, 0))
        total += jnp.where(lane == 0, 0.0, pltpu.roll(f, 1, 1))
        total += jnp.where(lane == NZ - 1, 0.0, pltpu.roll(f, NZ - 1, 1))
        return total

    def inside(src, squares):
        def body(x, carry):
            r = pl.multiple_of(8 * x, 8)
            total = zero_slab
            for q in range(Q):
                f = src[q, pl.ds(r + 8, 8), :]
                around = src[q, pl.ds(r, 8), :] + src[q, pl.ds(r + 16, 8), :]
                raw[q, pl.ds(r, 8), :] = around + sides(f, 0.0, 0.0)
                if squares:
                    total += f * f
            if squares:
                sq[pl.ds(r, 8), :] = total
            return carry

        lax.fori_loop(0, CX, body, 0)

    def add_faces(halo):
        for j in range(G):
            raw[j, 0:8, :] = raw[j, 0:8, :] + halo(0, j)
            raw[G + j, 56:64, :] = raw[G + j, 56:64, :] + halo(1, j)
            low, high = halo(2, j), halo(3, j)
            for x in range(CX):
                at = slice(8 * x, 8 * x + 8)
                row = jnp.where(sub == 0, low[x : x + 1, :], 0.0)
                raw[2 * G + j, at, :] = raw[2 * G + j, at, :] + row
                row = jnp.where(sub == CY - 1, high[x : x + 1, :], 0.0)
                raw[3 * G + j, at, :] = raw[3 * G + j, at, :] + row

    inside(u_ref, True)
    pl.semaphore_wait(token.at[1], len(twos))
    for o in group_xy:
        signal(token.at[2], torus_peer(*o))

    out_row = lax.broadcasted_iota(I32, (128, 192), 0)
    in_row = lax.broadcasted_iota(I32, (128, 192), 1) & 63
    high = out_row >> 3
    low = out_row & 7
    along = jnp.where(
        out_row < 64,
        high,
        jnp.where(out_row < 80, high - 10, jnp.where(out_row < 96, high - 2, low)),
    )
    across = jnp.where(out_row < 96, low, jnp.where(out_row < 112, high - 14, high - 6))

    def node_weight(fine, node):
        twice = 2 * fine - 1
        lower = twice >> 2
        w = (twice - 4 * lower).astype(F32) * 0.25
        return jnp.where(node == lower + 2, 1.0 - w, jnp.where(node == lower + 3, w, 0.0))

    weight_xy = node_weight(along, in_row >> 3) * node_weight(across, in_row & 7)
    node_z = lax.broadcasted_iota(I32, (3 * NZC, NZ), 0) & (NZC - 1)
    fine_z = lax.broadcasted_iota(I32, (3 * NZC, NZ), 1)
    lower_z = (2 * fine_z - 1) >> 2
    w_z = (2 * fine_z - 1 - 4 * lower_z).astype(F32) * 0.25
    weight_z = jnp.where(node_z == jnp.clip(lower_z, 0, NZC - 1), 1.0 - w_z, 0.0) + jnp.where(
        node_z == jnp.clip(lower_z + 1, 0, NZC - 1), w_z, 0.0
    )

    local[7].wait()
    wait_for(cb.at[pl.ds(0, 2 * CAP)], recv_sem.at[0])
    wait_for(cl, recv_sem.at[1])
    wait_for(cr, recv_sem.at[2])
    for i in range(8):
        plane = jnp.clip(s * (CX // 2) - 2 + i, 0, planes_all - 1)
        flat = jnp.where(
            plane < start_own,
            plane - start_prev,
            jnp.where(plane < end_own, CAP + plane - start_own, 2 * CAP + plane - end_own),
        )
        flat = jnp.clip(flat, 0, 3 * CAP - 1)
        mine = cb[flat]
        left = cl[flat, CYC - 2 : CYC, :]
        right = cr[flat, 0:2, :]
        pb[8 * i : 8 * i + 2, :] = jnp.where(c == 0, mine[0:1], left)
        pb[8 * i + 2 : 8 * i + 6, :] = mine
        pb[8 * i + 6 : 8 * i + 8, :] = jnp.where(c == cols - 1, mine[CYC - 1 : CYC], right)
    def three(value, axis):
        first = value.astype(BF16)
        rest = value - first.astype(F32)
        second = rest.astype(BF16)
        third = (rest - second.astype(F32)).astype(BF16)
        return jnp.concatenate([first, second, third], axis=axis)

    weight_xy = weight_xy.astype(BF16)
    weight_z = weight_z.astype(BF16)
    profile = jnp.dot(weight_xy, three(pb[...], 0), preferred_element_type=F32)
    profile = jnp.dot(three(profile, 1), weight_z, preferred_element_type=F32)
    scaled = TIME_STEP * jnp.exp(2.0 * (profile - 1.0))
    bf[0:64, :] = scaled[0:64] * mask[...].astype(F32)
    bf[64:128, :] = scaled[64:128]

    wait_for(rf, recv_sem.at[3])
    add_faces(lambda face, j: rf[face, j] * has[face])

    def near_b(face):
        at = 64 + 16 * face + 8 * near(face)
        return bf[at : at + 8, :]

    def react(src, dst, ready, shift, sums):
        def body(x, carry):
            r = pl.multiple_of(8 * x, 8)
            b = bf[pl.ds(r, 8), :]
            if shift is None:
                squares = sq[pl.ds(r, 8), :]
            else:
                m, extra = shift
                mb = m * b
                squares = st[0, pl.ds(r, 8), :] + mb * (16.0 * mb - 2.0 * st[1, pl.ds(r, 8), :])
                base = [extra + m * nbg[g, pl.ds(r, 8), :] for g in range(4)]
            common = 5.0 + 3.0 * squares
            acc = [zero_slab] * 6
            for q in range(Q):
                e = e_s[q]
                f = src[q, pl.ds(r + 8, 8), :]
                if shift is not None:
                    f = f - mb
                force = f * ((common - e) + f * (e - 2.0 * f))
                if sums and ready:
                    around = raw[q, pl.ds(r, 8), :]
                elif shift is None:
                    low_row = hy[0, q - 2 * G, pl.ds(x, 1), :] if q // G == 2 else 0.0
                    high_row = hy[1, q - 3 * G, pl.ds(x, 1), :] if q // G == 3 else 0.0
                    around = src[q, pl.ds(r, 8), :] + src[q, pl.ds(r + 16, 8), :]
                    around += sides(f, low_row, high_row)
                else:
                    around = raw[q, pl.ds(r, 8), :] - base[q // G]
                force = force - around
                a = f - b * force
                if sums:
                    square = a * a
                    ea = e * a
                    step = (force, a, square, square * a, ea, ea * a)
                    acc = [total + value for total, value in zip(acc, step)]
                elif dst is u_ref:
                    acc[0] += a * a
                dst[q, pl.ds(r + 8, 8), :] = a
            if not sums:
                if dst is u_ref:
                    sq[pl.ds(r, 8), :] = acc[0]
                return carry
            force_all, t1, t2, t3, te, te2 = acc
            st[0, pl.ds(r, 8), :] = t2
            st[1, pl.ds(r, 8), :] = t1
            total, k0, k1, k2 = carry
            b2 = b * b
            total += b * force_all
            k0 += b * (t1 * (5.0 + 3.0 * t2) - te + te2 - 2.0 * t3) - t1 * nbi[pl.ds(r, 8), :]
            k1 += b2 * (e_total - 80.0 - 42.0 * t2 - 6.0 * t1 * t1 - 2.0 * te)
            k2 += b2 * b * (138.0 * t1 + e_total)
            return total, k0, k1, k2

        start = (zero_slab,) * 4 if sums else 0
        return lax.fori_loop(0, CX, body, start)

    sum_b = zero_slab
    sum_b4 = zero_slab
    sum_bnb = zero_slab
    for x in range(CX):
        b = bf[8 * x : 8 * x + 8, :]
        around = sides(b, 0.0, 0.0)
        if x > 0:
            around += bf[8 * x - 8 : 8 * x, :]
        if x < CX - 1:
            around += bf[8 * x + 8 : 8 * x + 16, :]
        nbi[8 * x : 8 * x + 8, :] = around
        square = b * b
        sum_b += b
        sum_b4 += square * square
        sum_bnb += 16.0 * b * around

    parts = react(u_ref, v_ref, True, None, True)

    wait_for(rm, recv_sem.at[4])
    for face in range(4):
        at = 64 + 16 * face
        bf[at : at + 16, :] = bf[at : at + 16, :] * rm[face].astype(F32) * has[face]
    face_b = (bf[0:8, :], bf[56:64, :], column(bf, 0), column(bf, 7))
    for face in range(4):
        sum_bnb += 4.0 * face_b[face] * near_b(face)

    for j in range(G):
        for k in range(2):
            ya[0, j, 8 * k : 8 * k + 8, :] = column(v_ref.at[2 * G + j], 8 + k)
            ya[1, j, 8 * k : 8 * k + 8, :] = column(v_ref.at[3 * G + j], 14 + k)

    lane_1 = lax.broadcasted_iota(I32, (1, 128), 1)

    def put_row(at, parts, faces):
        total, k0, k1, k2 = parts
        for face in range(4):
            layer = faces[face][0]
            for j in range(1, G):
                layer = layer + faces[face][j]
            k0 -= layer * near_b(face)
        every = (sum_b, total, k0, k1 + sum_bnb, k2, -736.0 * sum_b4)
        tile = jnp.zeros((8, 128), F32)
        for k, part in enumerate(every):
            half = part[:, :128] + part[:, 128:]
            tile = jnp.where(sub[:, :128] == k, jnp.sum(half, axis=0, keepdims=True), tile)
        tile = jnp.where(sub[:, :128] == lane[:, :128], jnp.sum(tile, axis=1, keepdims=True), 0.0)
        row = jnp.sum(tile, axis=0, keepdims=True)
        ar_src[at] = row

    def spread(at, group, landing, sem):
        for k, offset in enumerate(group):
            send(ar_src.at[at], landing.at[k], torus_peer(*offset), sem)

    def gathered(at, landing, sem):
        wait_for(landing, recv_sem.at[sem])
        return ar_src[at] + jnp.sum(landing[...], axis=0)

    def two_multipliers(row):
        got = [
            jnp.sum(jnp.where(lane_1 == k, row, 0.0), axis=1, keepdims=True) for k in range(6)
        ]
        inverse = -1.0 / (16.0 * got[0])
        m_a = got[1] * inverse
        m_b = (got[2] + m_a * (got[3] + m_a * (got[4] + m_a * got[5]))) * inverse
        return jnp.broadcast_to(m_a, (CY, NZ)), jnp.broadcast_to(m_b, (CY, NZ))

    put_row(
        0,
        parts,
        (
            [v_ref[j, 8:16, :] for j in range(G)],
            [v_ref[G + j, 64:72, :] for j in range(G)],
            [ya[0, j, 0:8, :] for j in range(G)],
            [ya[1, j, 8:16, :] for j in range(G)],
        ),
    )
    pl.semaphore_wait(token.at[2], len(group_xy))
    spread(0, group_all, ar_1a, 5)

    for k in range(2):
        ys[0, k] = column(st.at[k], 0)
        ys[1, k] = column(st.at[k], 7)
    deep = (
        v_ref.at[pl.ds(0, G), pl.ds(8, 16)],
        v_ref.at[pl.ds(G, G), pl.ds(56, 16)],
        ya.at[0],
        ya.at[1],
    )
    flat = (st.at[:, pl.ds(0, 8)], st.at[:, pl.ds(56, 8)], ys.at[0], ys.at[1])
    for face in range(4):
        peer = halo_peer(*face_offset[face])
        send(deep[face], ra.at[face ^ 1], peer, 6)
        send(flat[face], rs.at[face ^ 1], peer, 7)
    inside(v_ref, False)
    for x in range(CX):
        at = slice(8 * x, 8 * x + 8)
        here = nbi[at, :]
        nbg[0, at, :] = here + near_b(0) if x == 0 else here
        nbg[1, at, :] = here + near_b(1) if x == CX - 1 else here
        nbg[2, at, :] = here + jnp.where(sub == 0, near_b(2)[x : x + 1, :], 0.0)
        nbg[3, at, :] = here + jnp.where(sub == CY - 1, near_b(3)[x : x + 1, :], 0.0)

    wait_for(ra, recv_sem.at[6])
    wait_for(rs, recv_sem.at[7])
    for face in range(4):
        here, beyond = 8 * near(face), 8 * (1 - near(face))
        at = 64 + 16 * face
        b = near_b(face)
        nbh[face] = bf[at + beyond : at + beyond + 8, :] + face_b[face] + sides(b, 0.0, 0.0)
        for j in range(G):
            value = ra[face, j, here : here + 8, :] * has[face]
            ah[face, j] = value
            if face == 0:
                inner = v_ref[j, 8:16, :]
            elif face == 1:
                inner = v_ref[G + j, 64:72, :]
            elif face == 2:
                inner = ya[0, j, 0:8, :]
            else:
                inner = ya[1, j, 8:16, :]
            outer = ra[face, j, beyond : beyond + 8, :]
            nh[face, j] = outer + inner + sides(value, 0.0, 0.0)
    add_faces(lambda face, j: ah[face, j])

    m0, m1 = two_multipliers(gathered(0, ar_1a, 5))

    wait_for(rf, send_sem.at[3])
    for face in range(4):
        b = near_b(face)
        mb = m0 * b
        squares = rs[face, 0] + mb * (16.0 * mb - 2.0 * rs[face, 1])
        common = 5.0 + 3.0 * squares
        base = m1 + m0 * nbh[face]
        for j in range(G):
            e = e_s[face * G + j]
            f = ah[face, j] - mb
            force = f * ((common - e) + f * (e - 2.0 * f)) - (nh[face, j] - base)
            value = f - b * force
            if face == 0:
                u_ref[j, 0:8, :] = value
            elif face == 1:
                u_ref[G + j, 72:80, :] = value
            else:
                hy[face - 2, j] = value
    react(v_ref, u_ref, True, (m0, m1), False)

    wait_for(ra, send_sem.at[6])
    wait_for(rs, send_sem.at[7])
    parts = react(u_ref, v_ref, False, None, True)
    for j in range(G):
        y2[0, j] = column(v_ref.at[2 * G + j], 8)
        y2[1, j] = column(v_ref.at[3 * G + j], 15)
    put_row(
        2,
        parts,
        (
            [v_ref[j, 8:16, :] for j in range(G)],
            [v_ref[G + j, 64:72, :] for j in range(G)],
            [y2[0, j] for j in range(G)],
            [y2[1, j] for j in range(G)],
        ),
    )
    spread(2, group_k, ar_2a, 9)
    ar_src[3] = gathered(2, ar_2a, 9)
    spread(3, group_xyz, ar_2b, 10)
    shallow = (
        v_ref.at[pl.ds(0, G), pl.ds(8, 8)],
        v_ref.at[pl.ds(G, G), pl.ds(64, 8)],
        y2.at[0],
        y2.at[1],
    )
    for face in range(4):
        send(shallow[face], r2.at[face ^ 1], halo_peer(*face_offset[face]), 11)
    inside(v_ref, False)
    wait_for(r2, recv_sem.at[11])
    add_faces(lambda face, j: r2[face, j] * has[face])
    wait_for(cb.at[pl.ds(0, 2 * CAP)], send_sem.at[0])
    wait_for(cl, send_sem.at[1])
    wait_for(cr, send_sem.at[2])
    wait_for(rm, send_sem.at[4])
    wait_for(ar_1a, send_sem.at[5])
    wait_for(ar_2a, send_sem.at[9])
    wait_for(r2, send_sem.at[11])

    def hand_over(x, carry):
        r = pl.multiple_of(8 * x, 8)
        for q in range(Q):
            p = pos_s[q]
            last_a[q, pl.ds(r, 8), :] = v_ref[p, pl.ds(r + 8, 8), :]
            last_n[q, pl.ds(r, 8), :] = raw[p, pl.ds(r, 8), :]
            last_b[q, pl.ds(r, 8), :] = nbg[p >> 2, pl.ds(r, 8), :]
        last_s[0, pl.ds(r, 8), :] = st[0, pl.ds(r, 8), :]
        last_s[1, pl.ds(r, 8), :] = st[1, pl.ds(r, 8), :]
        last_w[pl.ds(r, 8), :] = bf[pl.ds(r, 8), :]
        return carry

    lax.fori_loop(0, CX, hand_over, 0)
    for q in range(Q):
        last_e[q] = jnp.full((1, NZ), e_s[pos_s[q]], F32)

    m2, m3 = two_multipliers(gathered(3, ar_2b, 10))
    last_m[0] = m2
    last_m[1] = m3
    wait_for(ar_2b, send_sem.at[10])


def last_step(a_ref, n_ref, nb_ref, e_ref, s_ref, w_ref, m_ref, out_hbm, done, sem):
    m2 = m_ref[0]
    m3 = m_ref[1]
    copies = []
    for x in range(CX):
        at = slice(8 * x, 8 * x + 8)
        b = w_ref[at, :]
        mb = m2 * b
        common = 5.0 + 3.0 * (s_ref[0, at, :] + mb * (16.0 * mb - 2.0 * s_ref[1, at, :]))
        for q in range(Q):
            e = e_ref[q]
            f = a_ref[q, at, :] - mb
            around = n_ref[q, at, :] - (m3 + m2 * nb_ref[q, at, :])
            done[q, at, :] = f - b * (f * ((common - e) + f * (e - 2.0 * f)) - around)
        rows = pl.ds(8 * x, 8)
        copy = pltpu.make_async_copy(done.at[:, rows], out_hbm.at[:, rows], sem.at[x])
        copy.start()
        copies.append(copy)
    for copy in copies:
        copy.wait()


def per_device(torus, order_params, layer_mask, coarse_temp, coarse_rows, grain_ids, energy):
    any_space = pl.BlockSpec(memory_space=pl.ANY)
    vmem = pl.BlockSpec(memory_space=pltpu.VMEM)
    nx, nzt, ny, nk = torus
    slabs = nx * nzt
    rows = CX * CY

    handed_shapes = [(Q, rows, NZ)] * 3 + [(Q, 1, NZ), (2, rows, NZ), (rows, NZ), (2, CY, NZ)]

    def row_slots(count):
        return pltpu.VMEM((count, 1, 128), F32)

    handed = pl.pallas_call(
        functools.partial(kernel, torus),
        out_shape=tuple(pltpu.VMEM(shape, F32) for shape in handed_shapes),
        in_specs=[any_space] * 6,
        out_specs=(vmem,) * 7,
        scratch_shapes=[
            pltpu.VMEM((Q, rows, NZ), F32),
            pltpu.VMEM((rows, NZ), I32),
            pltpu.VMEM((3 * CAP, CYC, NZC), F32),
            pltpu.VMEM((3 * CAP, CYC, NZC), F32),
            pltpu.VMEM((3 * CAP, CYC, NZC), F32),
            pltpu.VMEM((64, NZC), F32),
            pltpu.VMEM((Q, rows + 16, NZ), F32),
            pltpu.VMEM((Q, rows + 16, NZ), F32),
            pltpu.VMEM((128, NZ), F32),
            pltpu.VMEM((rows, NZ), F32),
            pltpu.VMEM((4, rows, NZ), F32),
            pltpu.VMEM((4, 16, NZ), I32),
            pltpu.VMEM((2, 16, NZ), I32),
            pltpu.VMEM((2, G, 8, NZ), F32),
            pltpu.VMEM((4, G, 8, NZ), F32),
            pltpu.VMEM((2, G, 16, NZ), F32),
            pltpu.VMEM((4, G, 16, NZ), F32),
            pltpu.VMEM((2, rows, NZ), F32),
            pltpu.VMEM((2, 2, 8, NZ), F32),
            pltpu.VMEM((4, 2, 8, NZ), F32),
            pltpu.VMEM((rows, NZ), F32),
            pltpu.VMEM((2, G, 8, NZ), F32),
            pltpu.VMEM((4, G, 8, NZ), F32),
            pltpu.VMEM((4, G, 8, NZ), F32),
            pltpu.VMEM((4, 8, NZ), F32),
            pltpu.VMEM((2, G, 8, NZ), F32),
            pltpu.VMEM((4, G, 8, NZ), F32),
            row_slots(4),
            row_slots(nx * ny * nzt * nk - 1),
            row_slots(nk - 1),
            row_slots(nx * ny * nzt - 1),
            pltpu.SMEM((slabs,), I32),
            pltpu.VMEM((3, Q, slabs), I32),
            pltpu.SMEM((Q,), I32),
            pltpu.SMEM(energy.shape, F32),
            pltpu.SMEM((Q,), F32),
            pltpu.SMEM((Q,), I32),
            pltpu.SMEM((Q,), I32),
            pltpu.SemaphoreType.REGULAR((3,)),
            pltpu.SemaphoreType.DMA((8,)),
            pltpu.SemaphoreType.DMA((12,)),
            pltpu.SemaphoreType.DMA((12,)),
        ],
        compiler_params=pltpu.CompilerParams(collective_id=0, has_side_effects=True),
    )(
        coarse_rows,
        jnp.transpose(grain_ids, (1, 2, 0)),
        energy,
        order_params.reshape(Q, rows, NZ),
        layer_mask.reshape(rows, NZ),
        coarse_temp,
    )
    out = pl.pallas_call(
        last_step,
        out_shape=jax.ShapeDtypeStruct((Q, rows, NZ), F32),
        in_specs=[vmem] * 7,
        out_specs=any_space,
        scratch_shapes=[pltpu.VMEM((Q, rows, NZ), F32), pltpu.SemaphoreType.DMA((CX,))],
    )(*(pltpu.with_memory_space_constraint(part, pltpu.VMEM) for part in handed))
    return out.reshape(Q, CX, CY, NZ)


def solution(mesh, torus=(4, 8, 4, 2)):
    placed = (
        P(None, "slab", "col", None),
        P("slab", "col", None),
        P("slab", "col", None),
        P(),
        P(),
        P(),
    )
    return jax.shard_map(
        functools.partial(per_device, torus),
        mesh=mesh,
        in_specs=placed,
        out_specs=P(None, "slab", "col", None),
        check_vma=False,
    )
```

```python
import functools

import jax
import jax.numpy as jnp
from jax import lax
from jax.experimental import pallas as pl
from jax.experimental.pallas import tpu as pltpu
from jax.sharding import PartitionSpec as P

Q = 16
G = 4
CX = 8
CY = 8
NZ = 256
CAP = 6
CYC = 4
NZC = 128
TIME_STEP = 0.05
MESH = pl.DeviceIdType.MESH
F32 = jnp.float32
I32 = jnp.int32
BF16 = jnp.bfloat16


def near(face):
    return 1 if face in (0, 2) else 0


def wait_for(ref, sem):
    pltpu.make_async_copy(ref, ref, sem).wait()


def kernel(
    torus,
    rows_hbm,
    ids_hbm,
    energy_hbm,
    fields_hbm,
    mask_hbm,
    coarse_hbm,
    out_ref,
    raw,
    mask,
    cb,
    cl,
    cr,
    pb,
    u_ref,
    v_ref,
    bf,
    nbi,
    nbg,
    rm,
    ym,
    yf,
    rf,
    ya,
    ra,
    st,
    ys,
    rs,
    sq,
    hy,
    ah,
    nh,
    nbh,
    y2,
    r2,
    ar_src,
    ar_1a,
    ar_1b,
    ar_2a,
    ar_2b,
    rows_s,
    ids_v,
    ids_s,
    energy_s,
    e_s,
    perm_s,
    pos_s,
    token,
    local_sem,
    send_sem,
    recv_sem,
):
    nx, nzt, ny, nk = torus
    slabs, cols = nx * nzt, ny * nk
    s = lax.axis_index("slab")
    c = lax.axis_index("col")
    z_bits, k_bits = nzt.bit_length() - 1, nk.bit_length() - 1
    tx, tz = s >> z_bits, s & (nzt - 1)
    ty, tk = c >> k_bits, c & (nk - 1)
    planes_all = slabs * (CX // 2)
    col_low, col_high = jnp.maximum(c - 1, 0), jnp.minimum(c + 1, cols - 1)

    local = [
        pltpu.make_async_copy(ids_hbm.at[c], ids_v.at[0], local_sem.at[0]),
        pltpu.make_async_copy(ids_hbm.at[col_low], ids_v.at[1], local_sem.at[1]),
        pltpu.make_async_copy(ids_hbm.at[col_high], ids_v.at[2], local_sem.at[2]),
        pltpu.make_async_copy(energy_hbm, energy_s, local_sem.at[3]),
        pltpu.make_async_copy(rows_hbm, rows_s, local_sem.at[4]),
        pltpu.make_async_copy(fields_hbm, raw, local_sem.at[5]),
        pltpu.make_async_copy(mask_hbm, mask, local_sem.at[6]),
        pltpu.make_async_copy(coarse_hbm, cb.at[pl.ds(CAP, CAP)], local_sem.at[7]),
    ]
    for at in (5, 0, 1, 2):
        local[at].start()

    def halo_peer(ds, dc):
        return ((s + ds) & (slabs - 1), (c + dc) & (cols - 1))

    slab_part = [((tx + d) & (nx - 1)) << z_bits for d in range(nx)]
    z_part = [(tz + d) & (nzt - 1) for d in range(nzt)]
    y_part = [((ty + d) & (ny - 1)) << k_bits for d in range(ny)]
    k_part = [(tk + d) & (nk - 1) for d in range(nk)]

    def torus_peer(dx, dy, dz, dk):
        return (slab_part[dx] + z_part[dz], y_part[dy] + k_part[dk])

    def far(offset):
        return -sum(min(d, n - d) for d, n in zip(offset, (nx, ny, nzt, nk)))

    def offsets(sx, sy, sz, sk):
        every = [
            (a, b, d, e)
            for a in range(sx)
            for b in range(sy)
            for d in range(sz)
            for e in range(sk)
            if (a, b, d, e) != (0, 0, 0, 0)
        ]
        return sorted(every, key=far)

    halo_offsets = [(a, b) for a in (-1, 0, 1) for b in (-1, 0, 1) if (a, b) != (0, 0)]
    group_xy = offsets(nx, ny, 1, 1)
    group_k = offsets(1, 1, 1, nk)
    group_xyz = offsets(nx, ny, nzt, 1)

    def signal(sem, peer):
        pl.semaphore_signal(sem, inc=1, device_id=peer, device_id_type=MESH)

    steps = [(1, 0, 0), (nx - 1, 0, 0), (0, 1, 0), (0, ny - 1, 0), (0, 0, 1), (0, 0, nzt - 1)]
    peers = [halo_peer(*o) for o in halo_offsets]
    peers += [torus_peer(*o, 0) for o in steps]
    peers += [torus_peer(*o, 1) for o in steps[4:]]
    barrier = pltpu.get_barrier_semaphore()
    for peer in peers:
        signal(barrier, peer)
    for at in (6, 7, 4, 3):
        local[at].start()

    face_offset = ((-1, 0), (1, 0), (0, -1), (0, 1))
    has_flag = (s > 0, s < slabs - 1, c > 0, c < cols - 1)
    has = [jnp.where(flag, 1.0, 0.0).astype(F32) for flag in has_flag]

    def send(src, dst, peer, sem):
        pltpu.make_async_remote_copy(
            src_ref=src,
            dst_ref=dst,
            send_sem=send_sem.at[sem],
            recv_sem=recv_sem.at[sem],
            device_id=peer,
            device_id_type=MESH,
        ).start()

    sub = lax.broadcasted_iota(I32, (CY, NZ), 0)
    lane = lax.broadcasted_iota(I32, (CY, NZ), 1)
    zero_slab = jnp.zeros((CY, NZ), F32)

    def column(view, start):
        rows = jnp.broadcast_to(view[pl.ds(start, 1), :], (CX, NZ))
        for x in range(1, CX):
            rows = jnp.where(sub == x, view[pl.ds(start + CY * x, 1), :], rows)
        return rows

    sub_i = lax.broadcasted_iota(I32, (Q, 4 * Q), 0)
    lane_i = lax.broadcasted_iota(I32, (Q, 4 * Q), 1)
    lane_s = lax.broadcasted_iota(I32, (Q, slabs), 1)
    sub_q = lax.broadcasted_iota(I32, (Q, Q), 0)
    lane_q = lax.broadcasted_iota(I32, (Q, Q), 1)

    def ids_of(which, at):
        picked = jnp.where(lane_s == at, ids_v[which], 0)
        return jnp.sum(picked, axis=1, keepdims=True)

    def as_row(values):
        return jnp.sum(jnp.where(sub_q == lane_q, values, 0), axis=0, keepdims=True)

    for copy in local[:3]:
        copy.wait()
    own = ids_of(0, s)
    beside = (
        jnp.where(has_flag[0], ids_of(0, jnp.maximum(s - 1, 0)), -1),
        jnp.where(has_flag[1], ids_of(0, jnp.minimum(s + 1, slabs - 1)), -1),
        jnp.where(has_flag[2], ids_of(1, s), -1),
        jnp.where(has_flag[3], ids_of(2, s), -1),
    )
    face_i = lane_i >> 4
    every = jnp.where(
        face_i < 2,
        jnp.where(face_i == 0, beside[0], beside[1]),
        jnp.where(face_i == 2, beside[2], beside[3]),
    )
    every = jnp.sum(jnp.where((lane_i & 15) == sub_i, every, 0), axis=0, keepdims=True)
    found = jnp.sum(jnp.where(own == every, face_i + 1, 0), axis=1, keepdims=True)
    free = jnp.where(found == 0, own, 65535)
    free_rank = jnp.sum(jnp.where(as_row(free) < own, 1, 0), axis=1, keepdims=True)
    first_free = jnp.where(s == 0, 0, jnp.where(s == slabs - 1, 1, jnp.where(c == 0, 2, 3)))
    last_free = jnp.where(c == 0, 2, 3)
    place = jnp.where(free_rank < G, first_free, last_free)
    key = jnp.where(found == 0, place, found - 1) * 65536 + own
    position = jnp.sum(jnp.where(as_row(key) < key, 1, 0), axis=1, keepdims=True)
    order = jnp.sum(jnp.where(position == lane_q, sub_q, 0), axis=0, keepdims=True)
    order = jnp.minimum(order, Q - 1)
    own_row = as_row(own)
    position_row = as_row(position)
    for p in range(Q):
        perm_s[p] = order[0, p]

    pl.semaphore_wait(barrier, len(peers))
    for o in steps:
        signal(token.at[0], torus_peer(*o, 0))

    for ds, dc in halo_offsets:
        at = pl.ds((1 - ds) * CAP, CAP)
        if dc == 0:
            send(coarse_hbm, cb.at[at], halo_peer(ds, dc), 0)
        else:
            send(coarse_hbm, (cl if dc > 0 else cr).at[at], halo_peer(ds, dc), 1 if dc > 0 else 2)
    local[5].wait()
    for p in range(Q):
        u_ref[p, 8:72, :] = raw[perm_s[p]]
    for j in range(G):
        yf[0, j] = column(u_ref.at[2 * G + j], 8)
        yf[1, j] = column(u_ref.at[3 * G + j], 15)


    field_src = (
        u_ref.at[pl.ds(0, G), pl.ds(8, 8)],
        u_ref.at[pl.ds(G, G), pl.ds(64, 8)],
        yf.at[0],
        yf.at[1],
    )
    for face in range(4):
        send(field_src[face], rf.at[face ^ 1], halo_peer(*face_offset[face]), 3)
    local[6].wait()
    for k in range(2):
        ym[0, 8 * k : 8 * k + 8, :] = column(mask, k)
        ym[1, 8 * k : 8 * k + 8, :] = column(mask, 6 + k)
    mask_src = (mask.at[pl.ds(0, 16)], mask.at[pl.ds(48, 16)], ym.at[0], ym.at[1])
    for face in range(4):
        send(mask_src[face], rm.at[face ^ 1], halo_peer(*face_offset[face]), 4)

    for q in range(Q):
        for ref in (u_ref, v_ref):
            ref[q, 0:8, :] = zero_slab
            ref[q, 72:80, :] = zero_slab
    pl.semaphore_wait(token.at[0], len(steps))
    twos = [(2, 0, 0), (0, 2, 0), (0, 0, 2), (0, 0, nzt - 2)]
    for o in twos:
        signal(token.at[1], torus_peer(*o, 0))
    local[3].wait()
    for q in range(Q):
        pos_s[q] = position_row[0, q]
        ids_s[q] = own_row[0, q]
    for p in range(Q):
        e_s[p] = energy_s[ids_s[perm_s[p]]]
    e_total = e_s[0]
    for p in range(1, Q):
        e_total += e_s[p]
    local[4].wait()
    start_own = jnp.int32(0)
    for i in range(slabs):
        start_own += jnp.where(i < s, rows_s[i], 0)
    end_own = start_own + rows_s[s]
    start_prev = start_own - rows_s[jnp.maximum(s - 1, 0)]

    lane_h = lax.broadcasted_iota(I32, (CY, 128), 1)

    def sides(f, low_row, high_row):
        total = jnp.where(sub == 0, low_row, pltpu.roll(f, 1, 0))
        total += jnp.where(sub == CY - 1, high_row, pltpu.roll(f, CY - 1, 0))
        left, right = f[:, :128], f[:, 128:]
        left_up, right_up = pltpu.roll(left, 1, 1), pltpu.roll(right, 1, 1)
        left_down, right_down = pltpu.roll(left, 127, 1), pltpu.roll(right, 127, 1)
        first = jnp.where(lane_h == 0, 0.0, left_up) + jnp.where(
            lane_h == 127, right_down, left_down
        )
        second = jnp.where(lane_h == 0, left_up, right_up) + jnp.where(
            lane_h == 127, 0.0, right_down
        )
        return total + jnp.concatenate([first, second], axis=1)

    def inside(src, squares):
        def body(x, carry):
            r = pl.multiple_of(8 * x, 8)
            total = zero_slab
            for q in range(Q):
                f = src[q, pl.ds(r + 8, 8), :]
                around = src[q, pl.ds(r, 8), :] + src[q, pl.ds(r + 16, 8), :]
                raw[q, pl.ds(r, 8), :] = around + sides(f, 0.0, 0.0)
                if squares:
                    total += f * f
            if squares:
                sq[pl.ds(r, 8), :] = total
            return carry

        lax.fori_loop(0, CX, body, 0)

    def add_faces(halo):
        for j in range(G):
            raw[j, 0:8, :] = raw[j, 0:8, :] + halo(0, j)
            raw[G + j, 56:64, :] = raw[G + j, 56:64, :] + halo(1, j)
            low, high = halo(2, j), halo(3, j)
            for x in range(CX):
                at = slice(8 * x, 8 * x + 8)
                row = jnp.where(sub == 0, low[x : x + 1, :], 0.0)
                raw[2 * G + j, at, :] = raw[2 * G + j, at, :] + row
                row = jnp.where(sub == CY - 1, high[x : x + 1, :], 0.0)
                raw[3 * G + j, at, :] = raw[3 * G + j, at, :] + row

    inside(u_ref, True)
    pl.semaphore_wait(token.at[1], len(twos))
    for o in group_xy:
        signal(token.at[2], torus_peer(*o))

    out_row = lax.broadcasted_iota(I32, (128, 192), 0)
    in_row = lax.broadcasted_iota(I32, (128, 192), 1) & 63
    high = out_row >> 3
    low = out_row & 7
    along = jnp.where(
        out_row < 64,
        high,
        jnp.where(out_row < 80, high - 10, jnp.where(out_row < 96, high - 2, low)),
    )
    across = jnp.where(out_row < 96, low, jnp.where(out_row < 112, high - 14, high - 6))

    def node_weight(fine, node):
        twice = 2 * fine - 1
        lower = twice >> 2
        w = (twice - 4 * lower).astype(F32) * 0.25
        return jnp.where(node == lower + 2, 1.0 - w, jnp.where(node == lower + 3, w, 0.0))

    weight_xy = node_weight(along, in_row >> 3) * node_weight(across, in_row & 7)
    node_z = lax.broadcasted_iota(I32, (3 * NZC, NZ), 0) & (NZC - 1)
    fine_z = lax.broadcasted_iota(I32, (3 * NZC, NZ), 1)
    lower_z = (2 * fine_z - 1) >> 2
    w_z = (2 * fine_z - 1 - 4 * lower_z).astype(F32) * 0.25
    weight_z = jnp.where(node_z == jnp.clip(lower_z, 0, NZC - 1), 1.0 - w_z, 0.0) + jnp.where(
        node_z == jnp.clip(lower_z + 1, 0, NZC - 1), w_z, 0.0
    )
    weight_xy = weight_xy.astype(BF16)
    weight_z = weight_z.astype(BF16)

    local[7].wait()
    wait_for(cb.at[pl.ds(0, 2 * CAP)], recv_sem.at[0])
    wait_for(cl, recv_sem.at[1])
    wait_for(cr, recv_sem.at[2])
    for i in range(8):
        plane = jnp.clip(s * (CX // 2) - 2 + i, 0, planes_all - 1)
        flat = jnp.where(
            plane < start_own,
            plane - start_prev,
            jnp.where(plane < end_own, CAP + plane - start_own, 2 * CAP + plane - end_own),
        )
        flat = jnp.clip(flat, 0, 3 * CAP - 1)
        mine = cb[flat]
        left = cl[flat, CYC - 2 : CYC, :]
        right = cr[flat, 0:2, :]
        pb[8 * i : 8 * i + 2, :] = jnp.where(c == 0, mine[0:1], left)
        pb[8 * i + 2 : 8 * i + 6, :] = mine
        pb[8 * i + 6 : 8 * i + 8, :] = jnp.where(c == cols - 1, mine[CYC - 1 : CYC], right)
    def three(value, axis):
        first = value.astype(BF16)
        rest = value - first.astype(F32)
        second = rest.astype(BF16)
        third = (rest - second.astype(F32)).astype(BF16)
        return jnp.concatenate([first, second, third], axis=axis)

    profile = jnp.dot(weight_xy, three(pb[...], 0), preferred_element_type=F32)
    profile = jnp.dot(three(profile, 1), weight_z, preferred_element_type=F32)
    scaled = TIME_STEP * jnp.exp(2.0 * (profile - 1.0))
    bf[0:64, :] = scaled[0:64] * mask[...].astype(F32)
    bf[64:128, :] = scaled[64:128]

    wait_for(rf, recv_sem.at[3])
    add_faces(lambda face, j: rf[face, j] * has[face])

    def near_b(face):
        at = 64 + 16 * face + 8 * near(face)
        return bf[at : at + 8, :]

    def react(src, dst, offset, shift, sums):
        def body(x, carry):
            r = pl.multiple_of(8 * x, 8)
            b = bf[pl.ds(r, 8), :]
            if shift is None:
                squares = sq[pl.ds(r, 8), :]
            else:
                m, extra = shift
                mb = m * b
                squares = st[0, pl.ds(r, 8), :] + mb * (16.0 * mb - 2.0 * st[1, pl.ds(r, 8), :])
                base = [extra + m * nbg[g, pl.ds(r, 8), :] for g in range(4)]
            common = 5.0 + 3.0 * squares
            acc = [zero_slab] * 6
            for q in range(Q):
                p = pos_s[q] if dst is out_ref else q
                e = e_s[p]
                f = src[p, pl.ds(r + 8, 8), :]
                if shift is not None:
                    f = f - mb
                force = f * ((common - e) + f * (e - 2.0 * f))
                if sums and shift is None and src is not v_ref and offset is not None:
                    around = raw[q, pl.ds(r, 8), :]
                elif shift is None:
                    low_row = hy[0, q - 2 * G, pl.ds(x, 1), :] if q // G == 2 else 0.0
                    high_row = hy[1, q - 3 * G, pl.ds(x, 1), :] if q // G == 3 else 0.0
                    around = src[q, pl.ds(r, 8), :] + src[q, pl.ds(r + 16, 8), :]
                    around += sides(f, low_row, high_row)
                elif dst is out_ref:
                    around = raw[p, pl.ds(r, 8), :] - (extra + m * nbg[p >> 2, pl.ds(r, 8), :])
                else:
                    around = raw[q, pl.ds(r, 8), :] - base[q // G]
                force = force - around
                a = f - b * force
                if sums:
                    square = a * a
                    ea = e * a
                    step = (force, a, square, square * a, ea, ea * a)
                    acc = [total + value for total, value in zip(acc, step)]
                elif dst is u_ref:
                    acc[0] += a * a
                dst[q, pl.ds(r + (offset or 8 if dst is not out_ref else 0), 8), :] = a
            if not sums:
                if dst is u_ref:
                    sq[pl.ds(r, 8), :] = acc[0]
                return carry
            force_all, t1, t2, t3, te, te2 = acc
            st[0, pl.ds(r, 8), :] = t2
            st[1, pl.ds(r, 8), :] = t1
            total, k0, k1, k2 = carry
            b2 = b * b
            total += b * force_all
            k0 += b * (t1 * (5.0 + 3.0 * t2) - te + te2 - 2.0 * t3) - t1 * nbi[pl.ds(r, 8), :]
            k1 += b2 * (e_total - 80.0 - 42.0 * t2 - 6.0 * t1 * t1 - 2.0 * te)
            k2 += b2 * b * (138.0 * t1 + e_total)
            return total, k0, k1, k2

        start = (zero_slab,) * 4 if sums else 0
        return lax.fori_loop(0, CX, body, start, unroll=True)

    sum_b = zero_slab
    sum_b4 = zero_slab
    sum_bnb = zero_slab
    for x in range(CX):
        b = bf[8 * x : 8 * x + 8, :]
        around = sides(b, 0.0, 0.0)
        if x > 0:
            around += bf[8 * x - 8 : 8 * x, :]
        if x < CX - 1:
            around += bf[8 * x + 8 : 8 * x + 16, :]
        nbi[8 * x : 8 * x + 8, :] = around
        square = b * b
        sum_b += b
        sum_b4 += square * square
        sum_bnb += 16.0 * b * around

    parts = react(u_ref, v_ref, 8, None, True)

    wait_for(rm, recv_sem.at[4])
    for face in range(4):
        at = 64 + 16 * face
        bf[at : at + 16, :] = bf[at : at + 16, :] * rm[face].astype(F32) * has[face]
    face_b = (bf[0:8, :], bf[56:64, :], column(bf, 0), column(bf, 7))
    for face in range(4):
        sum_bnb += 4.0 * face_b[face] * near_b(face)

    for j in range(G):
        ya[0, j, 0:8, :] = column(v_ref.at[2 * G + j], 8)
        ya[1, j, 8:16, :] = column(v_ref.at[3 * G + j], 15)

    lane_1 = lax.broadcasted_iota(I32, (1, 128), 1)

    def put_row(at, parts, faces):
        total, k0, k1, k2 = parts
        for face in range(4):
            layer = faces[face][0]
            for j in range(1, G):
                layer = layer + faces[face][j]
            k0 -= layer * near_b(face)
        every = (sum_b, total, k0, k1 + sum_bnb, k2, -736.0 * sum_b4)
        tile = jnp.zeros((8, 128), F32)
        for k, part in enumerate(every):
            half = part[:, :128] + part[:, 128:]
            tile = jnp.where(sub[:, :128] == k, jnp.sum(half, axis=0, keepdims=True), tile)
        tile = jnp.where(sub[:, :128] == lane[:, :128], jnp.sum(tile, axis=1, keepdims=True), 0.0)
        row = jnp.sum(tile, axis=0, keepdims=True)
        ar_src[at] = row

    def spread(at, group, landing, sem):
        for k, offset in enumerate(group):
            send(ar_src.at[at], landing.at[k], torus_peer(*offset), sem)

    def gathered(at, landing, sem):
        wait_for(landing, recv_sem.at[sem])
        return ar_src[at] + jnp.sum(landing[...], axis=0)

    def two_multipliers(row):
        got = [
            jnp.sum(jnp.where(lane_1 == k, row, 0.0), axis=1, keepdims=True) for k in range(6)
        ]
        inverse = -1.0 / (16.0 * got[0])
        m_a = got[1] * inverse
        m_b = (got[2] + m_a * (got[3] + m_a * (got[4] + m_a * got[5]))) * inverse
        return jnp.broadcast_to(m_a, (CY, NZ)), jnp.broadcast_to(m_b, (CY, NZ))

    put_row(
        0,
        parts,
        (
            [v_ref[j, 8:16, :] for j in range(G)],
            [v_ref[G + j, 64:72, :] for j in range(G)],
            [ya[0, j, 0:8, :] for j in range(G)],
            [ya[1, j, 8:16, :] for j in range(G)],
        ),
    )
    spread(0, group_k, ar_1a, 5)

    for j in range(G):
        ya[0, j, 8:16, :] = column(v_ref.at[2 * G + j], 9)
        ya[1, j, 0:8, :] = column(v_ref.at[3 * G + j], 14)
    for k in range(2):
        ys[0, k] = column(st.at[k], 0)
        ys[1, k] = column(st.at[k], 7)
    pl.semaphore_wait(token.at[2], len(group_xy))
    ar_src[1] = gathered(0, ar_1a, 5)
    spread(1, group_xyz, ar_1b, 8)
    deep = (
        v_ref.at[pl.ds(0, G), pl.ds(8, 16)],
        v_ref.at[pl.ds(G, G), pl.ds(56, 16)],
        ya.at[0],
        ya.at[1],
    )
    flat = (st.at[:, pl.ds(0, 8)], st.at[:, pl.ds(56, 8)], ys.at[0], ys.at[1])
    for face in range(4):
        peer = halo_peer(*face_offset[face])
        send(deep[face], ra.at[face ^ 1], peer, 6)
        send(flat[face], rs.at[face ^ 1], peer, 7)
    inside(v_ref, False)
    for x in range(CX):
        at = slice(8 * x, 8 * x + 8)
        here = nbi[at, :]
        nbg[0, at, :] = here + near_b(0) if x == 0 else here
        nbg[1, at, :] = here + near_b(1) if x == CX - 1 else here
        nbg[2, at, :] = here + jnp.where(sub == 0, near_b(2)[x : x + 1, :], 0.0)
        nbg[3, at, :] = here + jnp.where(sub == CY - 1, near_b(3)[x : x + 1, :], 0.0)

    wait_for(ra, recv_sem.at[6])
    wait_for(rs, recv_sem.at[7])
    for face in range(4):
        here, beyond = 8 * near(face), 8 * (1 - near(face))
        at = 64 + 16 * face
        b = near_b(face)
        nbh[face] = bf[at + beyond : at + beyond + 8, :] + face_b[face] + sides(b, 0.0, 0.0)
        for j in range(G):
            value = ra[face, j, here : here + 8, :] * has[face]
            ah[face, j] = value
            if face == 0:
                inner = v_ref[j, 8:16, :]
            elif face == 1:
                inner = v_ref[G + j, 64:72, :]
            elif face == 2:
                inner = ya[0, j, 0:8, :]
            else:
                inner = ya[1, j, 8:16, :]
            outer = ra[face, j, beyond : beyond + 8, :]
            nh[face, j] = outer + inner + sides(value, 0.0, 0.0)
    add_faces(lambda face, j: ah[face, j])

    m0, m1 = two_multipliers(gathered(1, ar_1b, 8))

    wait_for(rf, send_sem.at[3])
    for face in range(4):
        b = near_b(face)
        mb = m0 * b
        squares = rs[face, 0] + mb * (16.0 * mb - 2.0 * rs[face, 1])
        common = 5.0 + 3.0 * squares
        base = m1 + m0 * nbh[face]
        for j in range(G):
            e = e_s[face * G + j]
            f = ah[face, j] - mb
            force = f * ((common - e) + f * (e - 2.0 * f)) - (nh[face, j] - base)
            value = f - b * force
            if face == 0:
                u_ref[j, 0:8, :] = value
            elif face == 1:
                u_ref[G + j, 72:80, :] = value
            else:
                hy[face - 2, j] = value
    react(v_ref, u_ref, 8, (m0, m1), False)

    wait_for(ra, send_sem.at[6])
    wait_for(rs, send_sem.at[7])
    parts = react(u_ref, v_ref, None, None, True)
    for j in range(G):
        y2[0, j] = column(v_ref.at[2 * G + j], 8)
        y2[1, j] = column(v_ref.at[3 * G + j], 15)
    put_row(
        2,
        parts,
        (
            [v_ref[j, 8:16, :] for j in range(G)],
            [v_ref[G + j, 64:72, :] for j in range(G)],
            [y2[0, j] for j in range(G)],
            [y2[1, j] for j in range(G)],
        ),
    )
    spread(2, group_k, ar_2a, 9)
    ar_src[3] = gathered(2, ar_2a, 9)
    spread(3, group_xyz, ar_2b, 10)
    shallow = (
        v_ref.at[pl.ds(0, G), pl.ds(8, 8)],
        v_ref.at[pl.ds(G, G), pl.ds(64, 8)],
        y2.at[0],
        y2.at[1],
    )
    for face in range(4):
        send(shallow[face], r2.at[face ^ 1], halo_peer(*face_offset[face]), 11)
    inside(v_ref, False)
    wait_for(r2, recv_sem.at[11])
    add_faces(lambda face, j: r2[face, j] * has[face])
    wait_for(cb.at[pl.ds(0, 2 * CAP)], send_sem.at[0])
    wait_for(cl, send_sem.at[1])
    wait_for(cr, send_sem.at[2])
    wait_for(rm, send_sem.at[4])
    wait_for(ar_1a, send_sem.at[5])
    wait_for(ar_1b, send_sem.at[8])
    wait_for(ar_2a, send_sem.at[9])
    wait_for(r2, send_sem.at[11])

    m2, m3 = two_multipliers(gathered(3, ar_2b, 10))
    react(v_ref, out_ref, 0, (m2, m3), False)
    wait_for(ar_2b, send_sem.at[10])


def write_out(result, out_hbm, sem):
    copy = pltpu.make_async_copy(result, out_hbm, sem.at[0])
    copy.start()
    copy.wait()


def per_device(torus, order_params, layer_mask, coarse_temp, coarse_rows, grain_ids, energy):
    any_space = pl.BlockSpec(memory_space=pl.ANY)
    vmem = pl.BlockSpec(memory_space=pltpu.VMEM)
    nx, nzt, ny, nk = torus
    slabs = nx * nzt
    rows = CX * CY

    def row_slots(count):
        return pltpu.VMEM((count, 1, 128), F32)

    result = pl.pallas_call(
        functools.partial(kernel, torus),
        out_shape=pltpu.VMEM((Q, rows, NZ), F32),
        in_specs=[any_space] * 6,
        out_specs=vmem,
        scratch_shapes=[
            pltpu.VMEM((Q, rows, NZ), F32),
            pltpu.VMEM((rows, NZ), I32),
            pltpu.VMEM((3 * CAP, CYC, NZC), F32),
            pltpu.VMEM((3 * CAP, CYC, NZC), F32),
            pltpu.VMEM((3 * CAP, CYC, NZC), F32),
            pltpu.VMEM((64, NZC), F32),
            pltpu.VMEM((Q, rows + 16, NZ), F32),
            pltpu.VMEM((Q, rows + 16, NZ), F32),
            pltpu.VMEM((128, NZ), F32),
            pltpu.VMEM((rows, NZ), F32),
            pltpu.VMEM((4, rows, NZ), F32),
            pltpu.VMEM((4, 16, NZ), I32),
            pltpu.VMEM((2, 16, NZ), I32),
            pltpu.VMEM((2, G, 8, NZ), F32),
            pltpu.VMEM((4, G, 8, NZ), F32),
            pltpu.VMEM((2, G, 16, NZ), F32),
            pltpu.VMEM((4, G, 16, NZ), F32),
            pltpu.VMEM((2, rows, NZ), F32),
            pltpu.VMEM((2, 2, 8, NZ), F32),
            pltpu.VMEM((4, 2, 8, NZ), F32),
            pltpu.VMEM((rows, NZ), F32),
            pltpu.VMEM((2, G, 8, NZ), F32),
            pltpu.VMEM((4, G, 8, NZ), F32),
            pltpu.VMEM((4, G, 8, NZ), F32),
            pltpu.VMEM((4, 8, NZ), F32),
            pltpu.VMEM((2, G, 8, NZ), F32),
            pltpu.VMEM((4, G, 8, NZ), F32),
            row_slots(4),
            row_slots(nk - 1),
            row_slots(nx * ny * nzt - 1),
            row_slots(nk - 1),
            row_slots(nx * ny * nzt - 1),
            pltpu.SMEM((slabs,), I32),
            pltpu.VMEM((3, Q, slabs), I32),
            pltpu.SMEM((Q,), I32),
            pltpu.SMEM(energy.shape, F32),
            pltpu.SMEM((Q,), F32),
            pltpu.SMEM((Q,), I32),
            pltpu.SMEM((Q,), I32),
            pltpu.SemaphoreType.REGULAR((3,)),
            pltpu.SemaphoreType.DMA((8,)),
            pltpu.SemaphoreType.DMA((12,)),
            pltpu.SemaphoreType.DMA((12,)),
        ],
        compiler_params=pltpu.CompilerParams(collective_id=0, has_side_effects=True),
    )(
        coarse_rows,
        jnp.transpose(grain_ids, (1, 2, 0)),
        energy,
        order_params.reshape(Q, rows, NZ),
        layer_mask.reshape(rows, NZ),
        coarse_temp,
    )
    out = pl.pallas_call(
        write_out,
        out_shape=jax.ShapeDtypeStruct((Q, rows, NZ), F32),
        in_specs=[vmem],
        out_specs=any_space,
        scratch_shapes=[pltpu.SemaphoreType.DMA((1,))],
    )(pltpu.with_memory_space_constraint(result, pltpu.VMEM))
    return out.reshape(Q, CX, CY, NZ)


def solution(mesh, torus=(4, 8, 4, 2)):
    placed = (
        P(None, "slab", "col", None),
        P("slab", "col", None),
        P("slab", "col", None),
        P(),
        P(),
        P(),
    )
    return jax.shard_map(
        functools.partial(per_device, torus),
        mesh=mesh,
        in_specs=placed,
        out_specs=P(None, "slab", "col", None),
        check_vma=False,
    )
```

```python
import functools

import jax
import jax.numpy as jnp
from jax import lax
from jax.experimental import pallas as pl
from jax.experimental.pallas import tpu as pltpu
from jax.sharding import PartitionSpec as P

Q = 16
G = 4
CX = 8
CY = 8
NZ = 256
CAP = 6
CYC = 4
NZC = 128
TIME_STEP = 0.05
MESH = pl.DeviceIdType.MESH
F32 = jnp.float32
I32 = jnp.int32
BF16 = jnp.bfloat16


def near(face):
    return 1 if face in (0, 2) else 0


def wait_for(ref, sem):
    pltpu.make_async_copy(ref, ref, sem).wait()


def kernel(
    torus,
    rows_hbm,
    ids_hbm,
    energy_hbm,
    fields_hbm,
    mask_hbm,
    coarse_hbm,
    last_a,
    last_n,
    last_b,
    last_e,
    last_s,
    last_w,
    last_m,
    raw,
    mask,
    cb,
    cl,
    cr,
    pb,
    u_ref,
    v_ref,
    bf,
    nbi,
    nbg,
    rm,
    ym,
    yf,
    rf,
    ya,
    ra,
    st,
    ys,
    rs,
    sq,
    hy,
    ah,
    nh,
    nbh,
    y2,
    r2,
    ar_src,
    ar_1a,
    ar_1b,
    ar_2a,
    ar_2b,
    rows_s,
    ids_v,
    ids_s,
    energy_s,
    e_s,
    perm_s,
    pos_s,
    token,
    local_sem,
    send_sem,
    recv_sem,
):
    nx, nzt, ny, nk = torus
    slabs, cols = nx * nzt, ny * nk
    s = lax.axis_index("slab")
    c = lax.axis_index("col")
    z_bits, k_bits = nzt.bit_length() - 1, nk.bit_length() - 1
    tx, tz = s >> z_bits, s & (nzt - 1)
    ty, tk = c >> k_bits, c & (nk - 1)
    planes_all = slabs * (CX // 2)
    col_low, col_high = jnp.maximum(c - 1, 0), jnp.minimum(c + 1, cols - 1)

    local = [
        pltpu.make_async_copy(ids_hbm.at[c], ids_v.at[0], local_sem.at[0]),
        pltpu.make_async_copy(ids_hbm.at[col_low], ids_v.at[1], local_sem.at[1]),
        pltpu.make_async_copy(ids_hbm.at[col_high], ids_v.at[2], local_sem.at[2]),
        pltpu.make_async_copy(energy_hbm, energy_s, local_sem.at[3]),
        pltpu.make_async_copy(rows_hbm, rows_s, local_sem.at[4]),
        pltpu.make_async_copy(fields_hbm, raw, local_sem.at[5]),
        pltpu.make_async_copy(mask_hbm, mask, local_sem.at[6]),
        pltpu.make_async_copy(coarse_hbm, cb.at[pl.ds(CAP, CAP)], local_sem.at[7]),
    ]
    for at in (5, 0, 1, 2):
        local[at].start()

    def halo_peer(ds, dc):
        return ((s + ds) & (slabs - 1), (c + dc) & (cols - 1))

    slab_part = [((tx + d) & (nx - 1)) << z_bits for d in range(nx)]
    z_part = [(tz + d) & (nzt - 1) for d in range(nzt)]
    y_part = [((ty + d) & (ny - 1)) << k_bits for d in range(ny)]
    k_part = [(tk + d) & (nk - 1) for d in range(nk)]

    def torus_peer(dx, dy, dz, dk):
        return (slab_part[dx] + z_part[dz], y_part[dy] + k_part[dk])

    def far(offset):
        return -sum(min(d, n - d) for d, n in zip(offset, (nx, ny, nzt, nk)))

    def offsets(sx, sy, sz, sk):
        every = [
            (a, b, d, e)
            for a in range(sx)
            for b in range(sy)
            for d in range(sz)
            for e in range(sk)
            if (a, b, d, e) != (0, 0, 0, 0)
        ]
        return sorted(every, key=far)

    halo_offsets = [(a, b) for a in (-1, 0, 1) for b in (-1, 0, 1) if (a, b) != (0, 0)]
    group_xy = offsets(nx, ny, 1, 1)
    group_k = offsets(1, 1, 1, nk)
    group_xyz = offsets(nx, ny, nzt, 1)

    def signal(sem, peer):
        pl.semaphore_signal(sem, inc=1, device_id=peer, device_id_type=MESH)

    steps = [(1, 0, 0), (nx - 1, 0, 0), (0, 1, 0), (0, ny - 1, 0), (0, 0, 1), (0, 0, nzt - 1)]
    peers = [halo_peer(*o) for o in halo_offsets]
    peers += [torus_peer(*o, 0) for o in steps]
    peers += [torus_peer(*o, 1) for o in steps[4:]]
    barrier = pltpu.get_barrier_semaphore()
    for peer in peers:
        signal(barrier, peer)
    for at in (6, 7, 4, 3):
        local[at].start()

    face_offset = ((-1, 0), (1, 0), (0, -1), (0, 1))
    has_flag = (s > 0, s < slabs - 1, c > 0, c < cols - 1)
    has = [jnp.where(flag, 1.0, 0.0).astype(F32) for flag in has_flag]

    def send(src, dst, peer, sem):
        pltpu.make_async_remote_copy(
            src_ref=src,
            dst_ref=dst,
            send_sem=send_sem.at[sem],
            recv_sem=recv_sem.at[sem],
            device_id=peer,
            device_id_type=MESH,
        ).start()

    sub = lax.broadcasted_iota(I32, (CY, NZ), 0)
    lane = lax.broadcasted_iota(I32, (CY, NZ), 1)
    zero_slab = jnp.zeros((CY, NZ), F32)

    def column(view, start):
        rows = jnp.broadcast_to(view[pl.ds(start, 1), :], (CX, NZ))
        for x in range(1, CX):
            rows = jnp.where(sub == x, view[pl.ds(start + CY * x, 1), :], rows)
        return rows

    sub_i = lax.broadcasted_iota(I32, (Q, 4 * Q), 0)
    lane_i = lax.broadcasted_iota(I32, (Q, 4 * Q), 1)
    lane_s = lax.broadcasted_iota(I32, (Q, slabs), 1)
    sub_q = lax.broadcasted_iota(I32, (Q, Q), 0)
    lane_q = lax.broadcasted_iota(I32, (Q, Q), 1)

    def ids_of(which, at):
        picked = jnp.where(lane_s == at, ids_v[which], 0)
        return jnp.sum(picked, axis=1, keepdims=True)

    def as_row(values):
        return jnp.sum(jnp.where(sub_q == lane_q, values, 0), axis=0, keepdims=True)

    for copy in local[:3]:
        copy.wait()
    own = ids_of(0, s)
    beside = (
        jnp.where(has_flag[0], ids_of(0, jnp.maximum(s - 1, 0)), -1),
        jnp.where(has_flag[1], ids_of(0, jnp.minimum(s + 1, slabs - 1)), -1),
        jnp.where(has_flag[2], ids_of(1, s), -1),
        jnp.where(has_flag[3], ids_of(2, s), -1),
    )
    face_i = lane_i >> 4
    every = jnp.where(
        face_i < 2,
        jnp.where(face_i == 0, beside[0], beside[1]),
        jnp.where(face_i == 2, beside[2], beside[3]),
    )
    every = jnp.sum(jnp.where((lane_i & 15) == sub_i, every, 0), axis=0, keepdims=True)
    found = jnp.sum(jnp.where(own == every, face_i + 1, 0), axis=1, keepdims=True)
    free = jnp.where(found == 0, own, 65535)
    free_rank = jnp.sum(jnp.where(as_row(free) < own, 1, 0), axis=1, keepdims=True)
    first_free = jnp.where(s == 0, 0, jnp.where(s == slabs - 1, 1, jnp.where(c == 0, 2, 3)))
    last_free = jnp.where(c == 0, 2, 3)
    place = jnp.where(free_rank < G, first_free, last_free)
    key = jnp.where(found == 0, place, found - 1) * 65536 + own
    position = jnp.sum(jnp.where(as_row(key) < key, 1, 0), axis=1, keepdims=True)
    order = jnp.sum(jnp.where(position == lane_q, sub_q, 0), axis=0, keepdims=True)
    order = jnp.minimum(order, Q - 1)
    own_row = as_row(own)
    position_row = as_row(position)
    for p in range(Q):
        perm_s[p] = order[0, p]

    pl.semaphore_wait(barrier, len(peers))
    for o in steps:
        signal(token.at[0], torus_peer(*o, 0))

    for ds, dc in halo_offsets:
        at = pl.ds((1 - ds) * CAP, CAP)
        if dc == 0:
            send(coarse_hbm, cb.at[at], halo_peer(ds, dc), 0)
        else:
            send(coarse_hbm, (cl if dc > 0 else cr).at[at], halo_peer(ds, dc), 1 if dc > 0 else 2)
    local[5].wait()
    for p in range(Q):
        u_ref[p, 8:72, :] = raw[perm_s[p]]
    for j in range(G):
        yf[0, j] = column(u_ref.at[2 * G + j], 8)
        yf[1, j] = column(u_ref.at[3 * G + j], 15)


    field_src = (
        u_ref.at[pl.ds(0, G), pl.ds(8, 8)],
        u_ref.at[pl.ds(G, G), pl.ds(64, 8)],
        yf.at[0],
        yf.at[1],
    )
    for face in range(4):
        send(field_src[face], rf.at[face ^ 1], halo_peer(*face_offset[face]), 3)
    local[6].wait()
    for k in range(2):
        ym[0, 8 * k : 8 * k + 8, :] = column(mask, k)
        ym[1, 8 * k : 8 * k + 8, :] = column(mask, 6 + k)
    mask_src = (mask.at[pl.ds(0, 16)], mask.at[pl.ds(48, 16)], ym.at[0], ym.at[1])
    for face in range(4):
        send(mask_src[face], rm.at[face ^ 1], halo_peer(*face_offset[face]), 4)

    for q in range(Q):
        for ref in (u_ref, v_ref):
            ref[q, 0:8, :] = zero_slab
            ref[q, 72:80, :] = zero_slab
    pl.semaphore_wait(token.at[0], len(steps))
    twos = [(2, 0, 0), (0, 2, 0), (0, 0, 2), (0, 0, nzt - 2)]
    for o in twos:
        signal(token.at[1], torus_peer(*o, 0))
    local[3].wait()
    for q in range(Q):
        pos_s[q] = position_row[0, q]
        ids_s[q] = own_row[0, q]
    for p in range(Q):
        e_s[p] = energy_s[ids_s[perm_s[p]]]
    e_total = e_s[0]
    for p in range(1, Q):
        e_total += e_s[p]
    local[4].wait()
    start_own = jnp.int32(0)
    for i in range(slabs):
        start_own += jnp.where(i < s, rows_s[i], 0)
    end_own = start_own + rows_s[s]
    start_prev = start_own - rows_s[jnp.maximum(s - 1, 0)]

    lane_h = lax.broadcasted_iota(I32, (CY, 128), 1)

    def sides(f, low_row, high_row):
        total = jnp.where(sub == 0, low_row, pltpu.roll(f, 1, 0))
        total += jnp.where(sub == CY - 1, high_row, pltpu.roll(f, CY - 1, 0))
        left, right = f[:, :128], f[:, 128:]
        left_up, right_up = pltpu.roll(left, 1, 1), pltpu.roll(right, 1, 1)
        left_down, right_down = pltpu.roll(left, 127, 1), pltpu.roll(right, 127, 1)
        first = jnp.where(lane_h == 0, 0.0, left_up) + jnp.where(
            lane_h == 127, right_down, left_down
        )
        second = jnp.where(lane_h == 0, left_up, right_up) + jnp.where(
            lane_h == 127, 0.0, right_down
        )
        return total + jnp.concatenate([first, second], axis=1)

    def inside(src, squares):
        def body(x, carry):
            r = pl.multiple_of(8 * x, 8)
            total = zero_slab
            for q in range(Q):
                f = src[q, pl.ds(r + 8, 8), :]
                around = src[q, pl.ds(r, 8), :] + src[q, pl.ds(r + 16, 8), :]
                raw[q, pl.ds(r, 8), :] = around + sides(f, 0.0, 0.0)
                if squares:
                    total += f * f
            if squares:
                sq[pl.ds(r, 8), :] = total
            return carry

        lax.fori_loop(0, CX, body, 0)

    def add_faces(halo):
        for j in range(G):
            raw[j, 0:8, :] = raw[j, 0:8, :] + halo(0, j)
            raw[G + j, 56:64, :] = raw[G + j, 56:64, :] + halo(1, j)
            low, high = halo(2, j), halo(3, j)
            for x in range(CX):
                at = slice(8 * x, 8 * x + 8)
                row = jnp.where(sub == 0, low[x : x + 1, :], 0.0)
                raw[2 * G + j, at, :] = raw[2 * G + j, at, :] + row
                row = jnp.where(sub == CY - 1, high[x : x + 1, :], 0.0)
                raw[3 * G + j, at, :] = raw[3 * G + j, at, :] + row

    inside(u_ref, True)
    pl.semaphore_wait(token.at[1], len(twos))
    for o in group_xy:
        signal(token.at[2], torus_peer(*o))

    out_row = lax.broadcasted_iota(I32, (128, 192), 0)
    in_row = lax.broadcasted_iota(I32, (128, 192), 1) & 63
    high = out_row >> 3
    low = out_row & 7
    along = jnp.where(
        out_row < 64,
        high,
        jnp.where(out_row < 80, high - 10, jnp.where(out_row < 96, high - 2, low)),
    )
    across = jnp.where(out_row < 96, low, jnp.where(out_row < 112, high - 14, high - 6))

    def node_weight(fine, node):
        twice = 2 * fine - 1
        lower = twice >> 2
        w = (twice - 4 * lower).astype(F32) * 0.25
        return jnp.where(node == lower + 2, 1.0 - w, jnp.where(node == lower + 3, w, 0.0))

    weight_xy = node_weight(along, in_row >> 3) * node_weight(across, in_row & 7)
    node_z = lax.broadcasted_iota(I32, (3 * NZC, NZ), 0) & (NZC - 1)
    fine_z = lax.broadcasted_iota(I32, (3 * NZC, NZ), 1)
    lower_z = (2 * fine_z - 1) >> 2
    w_z = (2 * fine_z - 1 - 4 * lower_z).astype(F32) * 0.25
    weight_z = jnp.where(node_z == jnp.clip(lower_z, 0, NZC - 1), 1.0 - w_z, 0.0) + jnp.where(
        node_z == jnp.clip(lower_z + 1, 0, NZC - 1), w_z, 0.0
    )
    weight_xy = weight_xy.astype(BF16)
    weight_z = weight_z.astype(BF16)

    local[7].wait()
    wait_for(cb.at[pl.ds(0, 2 * CAP)], recv_sem.at[0])
    wait_for(cl, recv_sem.at[1])
    wait_for(cr, recv_sem.at[2])
    for i in range(8):
        plane = jnp.clip(s * (CX // 2) - 2 + i, 0, planes_all - 1)
        flat = jnp.where(
            plane < start_own,
            plane - start_prev,
            jnp.where(plane < end_own, CAP + plane - start_own, 2 * CAP + plane - end_own),
        )
        flat = jnp.clip(flat, 0, 3 * CAP - 1)
        mine = cb[flat]
        left = cl[flat, CYC - 2 : CYC, :]
        right = cr[flat, 0:2, :]
        pb[8 * i : 8 * i + 2, :] = jnp.where(c == 0, mine[0:1], left)
        pb[8 * i + 2 : 8 * i + 6, :] = mine
        pb[8 * i + 6 : 8 * i + 8, :] = jnp.where(c == cols - 1, mine[CYC - 1 : CYC], right)
    def three(value, axis):
        first = value.astype(BF16)
        rest = value - first.astype(F32)
        second = rest.astype(BF16)
        third = (rest - second.astype(F32)).astype(BF16)
        return jnp.concatenate([first, second, third], axis=axis)

    profile = jnp.dot(weight_xy, three(pb[...], 0), preferred_element_type=F32)
    profile = jnp.dot(three(profile, 1), weight_z, preferred_element_type=F32)
    scaled = TIME_STEP * jnp.exp(2.0 * (profile - 1.0))
    bf[0:64, :] = scaled[0:64] * mask[...].astype(F32)
    bf[64:128, :] = scaled[64:128]

    wait_for(rf, recv_sem.at[3])
    add_faces(lambda face, j: rf[face, j] * has[face])

    def near_b(face):
        at = 64 + 16 * face + 8 * near(face)
        return bf[at : at + 8, :]

    def react(src, dst, ready, shift, sums):
        def body(x, carry):
            r = pl.multiple_of(8 * x, 8)
            b = bf[pl.ds(r, 8), :]
            if shift is None:
                squares = sq[pl.ds(r, 8), :]
            else:
                m, extra = shift
                mb = m * b
                squares = st[0, pl.ds(r, 8), :] + mb * (16.0 * mb - 2.0 * st[1, pl.ds(r, 8), :])
                base = [extra + m * nbg[g, pl.ds(r, 8), :] for g in range(4)]
            common = 5.0 + 3.0 * squares
            acc = [zero_slab] * 6
            for q in range(Q):
                e = e_s[q]
                f = src[q, pl.ds(r + 8, 8), :]
                if shift is not None:
                    f = f - mb
                force = f * ((common - e) + f * (e - 2.0 * f))
                if sums and ready:
                    around = raw[q, pl.ds(r, 8), :]
                elif shift is None:
                    low_row = hy[0, q - 2 * G, pl.ds(x, 1), :] if q // G == 2 else 0.0
                    high_row = hy[1, q - 3 * G, pl.ds(x, 1), :] if q // G == 3 else 0.0
                    around = src[q, pl.ds(r, 8), :] + src[q, pl.ds(r + 16, 8), :]
                    around += sides(f, low_row, high_row)
                else:
                    around = raw[q, pl.ds(r, 8), :] - base[q // G]
                force = force - around
                a = f - b * force
                if sums:
                    square = a * a
                    ea = e * a
                    step = (force, a, square, square * a, ea, ea * a)
                    acc = [total + value for total, value in zip(acc, step)]
                elif dst is u_ref:
                    acc[0] += a * a
                dst[q, pl.ds(r + 8, 8), :] = a
            if not sums:
                if dst is u_ref:
                    sq[pl.ds(r, 8), :] = acc[0]
                return carry
            force_all, t1, t2, t3, te, te2 = acc
            st[0, pl.ds(r, 8), :] = t2
            st[1, pl.ds(r, 8), :] = t1
            total, k0, k1, k2 = carry
            b2 = b * b
            total += b * force_all
            k0 += b * (t1 * (5.0 + 3.0 * t2) - te + te2 - 2.0 * t3) - t1 * nbi[pl.ds(r, 8), :]
            k1 += b2 * (e_total - 80.0 - 42.0 * t2 - 6.0 * t1 * t1 - 2.0 * te)
            k2 += b2 * b * (138.0 * t1 + e_total)
            return total, k0, k1, k2

        start = (zero_slab,) * 4 if sums else 0
        return lax.fori_loop(0, CX, body, start, unroll=True)

    sum_b = zero_slab
    sum_b4 = zero_slab
    sum_bnb = zero_slab
    for x in range(CX):
        b = bf[8 * x : 8 * x + 8, :]
        around = sides(b, 0.0, 0.0)
        if x > 0:
            around += bf[8 * x - 8 : 8 * x, :]
        if x < CX - 1:
            around += bf[8 * x + 8 : 8 * x + 16, :]
        nbi[8 * x : 8 * x + 8, :] = around
        square = b * b
        sum_b += b
        sum_b4 += square * square
        sum_bnb += 16.0 * b * around

    parts = react(u_ref, v_ref, True, None, True)

    wait_for(rm, recv_sem.at[4])
    for face in range(4):
        at = 64 + 16 * face
        bf[at : at + 16, :] = bf[at : at + 16, :] * rm[face].astype(F32) * has[face]
    face_b = (bf[0:8, :], bf[56:64, :], column(bf, 0), column(bf, 7))
    for face in range(4):
        sum_bnb += 4.0 * face_b[face] * near_b(face)

    for j in range(G):
        ya[0, j, 0:8, :] = column(v_ref.at[2 * G + j], 8)
        ya[1, j, 8:16, :] = column(v_ref.at[3 * G + j], 15)

    lane_1 = lax.broadcasted_iota(I32, (1, 128), 1)

    def put_row(at, parts, faces):
        total, k0, k1, k2 = parts
        for face in range(4):
            layer = faces[face][0]
            for j in range(1, G):
                layer = layer + faces[face][j]
            k0 -= layer * near_b(face)
        every = (sum_b, total, k0, k1 + sum_bnb, k2, -736.0 * sum_b4)
        tile = jnp.zeros((8, 128), F32)
        for k, part in enumerate(every):
            half = part[:, :128] + part[:, 128:]
            tile = jnp.where(sub[:, :128] == k, jnp.sum(half, axis=0, keepdims=True), tile)
        tile = jnp.where(sub[:, :128] == lane[:, :128], jnp.sum(tile, axis=1, keepdims=True), 0.0)
        row = jnp.sum(tile, axis=0, keepdims=True)
        ar_src[at] = row

    def spread(at, group, landing, sem):
        for k, offset in enumerate(group):
            send(ar_src.at[at], landing.at[k], torus_peer(*offset), sem)

    def gathered(at, landing, sem):
        wait_for(landing, recv_sem.at[sem])
        return ar_src[at] + jnp.sum(landing[...], axis=0)

    def two_multipliers(row):
        got = [
            jnp.sum(jnp.where(lane_1 == k, row, 0.0), axis=1, keepdims=True) for k in range(6)
        ]
        inverse = -1.0 / (16.0 * got[0])
        m_a = got[1] * inverse
        m_b = (got[2] + m_a * (got[3] + m_a * (got[4] + m_a * got[5]))) * inverse
        return jnp.broadcast_to(m_a, (CY, NZ)), jnp.broadcast_to(m_b, (CY, NZ))

    put_row(
        0,
        parts,
        (
            [v_ref[j, 8:16, :] for j in range(G)],
            [v_ref[G + j, 64:72, :] for j in range(G)],
            [ya[0, j, 0:8, :] for j in range(G)],
            [ya[1, j, 8:16, :] for j in range(G)],
        ),
    )
    spread(0, group_k, ar_1a, 5)

    for j in range(G):
        ya[0, j, 8:16, :] = column(v_ref.at[2 * G + j], 9)
        ya[1, j, 0:8, :] = column(v_ref.at[3 * G + j], 14)
    for k in range(2):
        ys[0, k] = column(st.at[k], 0)
        ys[1, k] = column(st.at[k], 7)
    pl.semaphore_wait(token.at[2], len(group_xy))
    ar_src[1] = gathered(0, ar_1a, 5)
    spread(1, group_xyz, ar_1b, 8)
    deep = (
        v_ref.at[pl.ds(0, G), pl.ds(8, 16)],
        v_ref.at[pl.ds(G, G), pl.ds(56, 16)],
        ya.at[0],
        ya.at[1],
    )
    flat = (st.at[:, pl.ds(0, 8)], st.at[:, pl.ds(56, 8)], ys.at[0], ys.at[1])
    for face in range(4):
        peer = halo_peer(*face_offset[face])
        send(deep[face], ra.at[face ^ 1], peer, 6)
        send(flat[face], rs.at[face ^ 1], peer, 7)
    inside(v_ref, False)
    for x in range(CX):
        at = slice(8 * x, 8 * x + 8)
        here = nbi[at, :]
        nbg[0, at, :] = here + near_b(0) if x == 0 else here
        nbg[1, at, :] = here + near_b(1) if x == CX - 1 else here
        nbg[2, at, :] = here + jnp.where(sub == 0, near_b(2)[x : x + 1, :], 0.0)
        nbg[3, at, :] = here + jnp.where(sub == CY - 1, near_b(3)[x : x + 1, :], 0.0)

    wait_for(ra, recv_sem.at[6])
    wait_for(rs, recv_sem.at[7])
    for face in range(4):
        here, beyond = 8 * near(face), 8 * (1 - near(face))
        at = 64 + 16 * face
        b = near_b(face)
        nbh[face] = bf[at + beyond : at + beyond + 8, :] + face_b[face] + sides(b, 0.0, 0.0)
        for j in range(G):
            value = ra[face, j, here : here + 8, :] * has[face]
            ah[face, j] = value
            if face == 0:
                inner = v_ref[j, 8:16, :]
            elif face == 1:
                inner = v_ref[G + j, 64:72, :]
            elif face == 2:
                inner = ya[0, j, 0:8, :]
            else:
                inner = ya[1, j, 8:16, :]
            outer = ra[face, j, beyond : beyond + 8, :]
            nh[face, j] = outer + inner + sides(value, 0.0, 0.0)
    add_faces(lambda face, j: ah[face, j])

    m0, m1 = two_multipliers(gathered(1, ar_1b, 8))

    wait_for(rf, send_sem.at[3])
    for face in range(4):
        b = near_b(face)
        mb = m0 * b
        squares = rs[face, 0] + mb * (16.0 * mb - 2.0 * rs[face, 1])
        common = 5.0 + 3.0 * squares
        base = m1 + m0 * nbh[face]
        for j in range(G):
            e = e_s[face * G + j]
            f = ah[face, j] - mb
            force = f * ((common - e) + f * (e - 2.0 * f)) - (nh[face, j] - base)
            value = f - b * force
            if face == 0:
                u_ref[j, 0:8, :] = value
            elif face == 1:
                u_ref[G + j, 72:80, :] = value
            else:
                hy[face - 2, j] = value
    react(v_ref, u_ref, True, (m0, m1), False)

    wait_for(ra, send_sem.at[6])
    wait_for(rs, send_sem.at[7])
    parts = react(u_ref, v_ref, False, None, True)
    for j in range(G):
        y2[0, j] = column(v_ref.at[2 * G + j], 8)
        y2[1, j] = column(v_ref.at[3 * G + j], 15)
    put_row(
        2,
        parts,
        (
            [v_ref[j, 8:16, :] for j in range(G)],
            [v_ref[G + j, 64:72, :] for j in range(G)],
            [y2[0, j] for j in range(G)],
            [y2[1, j] for j in range(G)],
        ),
    )
    spread(2, group_k, ar_2a, 9)
    ar_src[3] = gathered(2, ar_2a, 9)
    spread(3, group_xyz, ar_2b, 10)
    shallow = (
        v_ref.at[pl.ds(0, G), pl.ds(8, 8)],
        v_ref.at[pl.ds(G, G), pl.ds(64, 8)],
        y2.at[0],
        y2.at[1],
    )
    for face in range(4):
        send(shallow[face], r2.at[face ^ 1], halo_peer(*face_offset[face]), 11)
    inside(v_ref, False)
    wait_for(r2, recv_sem.at[11])
    add_faces(lambda face, j: r2[face, j] * has[face])
    wait_for(cb.at[pl.ds(0, 2 * CAP)], send_sem.at[0])
    wait_for(cl, send_sem.at[1])
    wait_for(cr, send_sem.at[2])
    wait_for(rm, send_sem.at[4])
    wait_for(ar_1a, send_sem.at[5])
    wait_for(ar_1b, send_sem.at[8])
    wait_for(ar_2a, send_sem.at[9])
    wait_for(r2, send_sem.at[11])

    def hand_over(x, carry):
        r = pl.multiple_of(8 * x, 8)
        for q in range(Q):
            p = pos_s[q]
            last_a[q, pl.ds(r, 8), :] = v_ref[p, pl.ds(r + 8, 8), :]
            last_n[q, pl.ds(r, 8), :] = raw[p, pl.ds(r, 8), :]
            last_b[q, pl.ds(r, 8), :] = nbg[p >> 2, pl.ds(r, 8), :]
        last_s[0, pl.ds(r, 8), :] = st[0, pl.ds(r, 8), :]
        last_s[1, pl.ds(r, 8), :] = st[1, pl.ds(r, 8), :]
        last_w[pl.ds(r, 8), :] = bf[pl.ds(r, 8), :]
        return carry

    lax.fori_loop(0, CX, hand_over, 0)
    for q in range(Q):
        last_e[q] = jnp.full((1, NZ), e_s[pos_s[q]], F32)

    m2, m3 = two_multipliers(gathered(3, ar_2b, 10))
    last_m[0] = m2
    last_m[1] = m3
    wait_for(ar_2b, send_sem.at[10])


def last_step(a_ref, n_ref, nb_ref, e_ref, s_ref, w_ref, m_ref, out_hbm, done, sem):
    m2 = m_ref[0]
    m3 = m_ref[1]

    def body(x, carry):
        at = pl.ds(pl.multiple_of(8 * x, 8), 8)
        b = w_ref[at, :]
        mb = m2 * b
        common = 5.0 + 3.0 * (s_ref[0, at, :] + mb * (16.0 * mb - 2.0 * s_ref[1, at, :]))
        for q in range(Q):
            e = e_ref[q]
            f = a_ref[q, at, :] - mb
            around = n_ref[q, at, :] - (m3 + m2 * nb_ref[q, at, :])
            done[q, at, :] = f - b * (f * ((common - e) + f * (e - 2.0 * f)) - around)
        pltpu.make_async_copy(done.at[:, at], out_hbm.at[:, at], sem.at[x]).start()
        return carry

    lax.fori_loop(0, CX, body, 0)
    for x in range(CX):
        rows = pl.ds(8 * x, 8)
        pltpu.make_async_copy(done.at[:, rows], out_hbm.at[:, rows], sem.at[x]).wait()


def per_device(torus, order_params, layer_mask, coarse_temp, coarse_rows, grain_ids, energy):
    any_space = pl.BlockSpec(memory_space=pl.ANY)
    vmem = pl.BlockSpec(memory_space=pltpu.VMEM)
    nx, nzt, ny, nk = torus
    slabs = nx * nzt
    rows = CX * CY

    handed_shapes = [(Q, rows, NZ)] * 3 + [(Q, 1, NZ), (2, rows, NZ), (rows, NZ), (2, CY, NZ)]

    def row_slots(count):
        return pltpu.VMEM((count, 1, 128), F32)

    handed = pl.pallas_call(
        functools.partial(kernel, torus),
        out_shape=tuple(pltpu.VMEM(shape, F32) for shape in handed_shapes),
        in_specs=[any_space] * 6,
        out_specs=(vmem,) * 7,
        scratch_shapes=[
            pltpu.VMEM((Q, rows, NZ), F32),
            pltpu.VMEM((rows, NZ), I32),
            pltpu.VMEM((3 * CAP, CYC, NZC), F32),
            pltpu.VMEM((3 * CAP, CYC, NZC), F32),
            pltpu.VMEM((3 * CAP, CYC, NZC), F32),
            pltpu.VMEM((64, NZC), F32),
            pltpu.VMEM((Q, rows + 16, NZ), F32),
            pltpu.VMEM((Q, rows + 16, NZ), F32),
            pltpu.VMEM((128, NZ), F32),
            pltpu.VMEM((rows, NZ), F32),
            pltpu.VMEM((4, rows, NZ), F32),
            pltpu.VMEM((4, 16, NZ), I32),
            pltpu.VMEM((2, 16, NZ), I32),
            pltpu.VMEM((2, G, 8, NZ), F32),
            pltpu.VMEM((4, G, 8, NZ), F32),
            pltpu.VMEM((2, G, 16, NZ), F32),
            pltpu.VMEM((4, G, 16, NZ), F32),
            pltpu.VMEM((2, rows, NZ), F32),
            pltpu.VMEM((2, 2, 8, NZ), F32),
            pltpu.VMEM((4, 2, 8, NZ), F32),
            pltpu.VMEM((rows, NZ), F32),
            pltpu.VMEM((2, G, 8, NZ), F32),
            pltpu.VMEM((4, G, 8, NZ), F32),
            pltpu.VMEM((4, G, 8, NZ), F32),
            pltpu.VMEM((4, 8, NZ), F32),
            pltpu.VMEM((2, G, 8, NZ), F32),
            pltpu.VMEM((4, G, 8, NZ), F32),
            row_slots(4),
            row_slots(nk - 1),
            row_slots(nx * ny * nzt - 1),
            row_slots(nk - 1),
            row_slots(nx * ny * nzt - 1),
            pltpu.SMEM((slabs,), I32),
            pltpu.VMEM((3, Q, slabs), I32),
            pltpu.SMEM((Q,), I32),
            pltpu.SMEM(energy.shape, F32),
            pltpu.SMEM((Q,), F32),
            pltpu.SMEM((Q,), I32),
            pltpu.SMEM((Q,), I32),
            pltpu.SemaphoreType.REGULAR((3,)),
            pltpu.SemaphoreType.DMA((8,)),
            pltpu.SemaphoreType.DMA((12,)),
            pltpu.SemaphoreType.DMA((12,)),
        ],
        compiler_params=pltpu.CompilerParams(collective_id=0, has_side_effects=True),
    )(
        coarse_rows,
        jnp.transpose(grain_ids, (1, 2, 0)),
        energy,
        order_params.reshape(Q, rows, NZ),
        layer_mask.reshape(rows, NZ),
        coarse_temp,
    )
    out = pl.pallas_call(
        last_step,
        out_shape=jax.ShapeDtypeStruct((Q, rows, NZ), F32),
        in_specs=[vmem] * 7,
        out_specs=any_space,
        scratch_shapes=[pltpu.VMEM((Q, rows, NZ), F32), pltpu.SemaphoreType.DMA((CX,))],
    )(*(pltpu.with_memory_space_constraint(part, pltpu.VMEM) for part in handed))
    return out.reshape(Q, CX, CY, NZ)


def solution(mesh, torus=(4, 8, 4, 2)):
    placed = (
        P(None, "slab", "col", None),
        P("slab", "col", None),
        P("slab", "col", None),
        P(),
        P(),
        P(),
    )
    return jax.shard_map(
        functools.partial(per_device, torus),
        mesh=mesh,
        in_specs=placed,
        out_specs=P(None, "slab", "col", None),
        check_vma=False,
    )
```
